512 devices in a mesh: row: 4 (over y_hi, core), sector: 64 (over z, x), band: 2 (over y_lo).
Axes of the slice: x: 4, y: 4 (y_hi: 2, y_lo: 2; y = y_hi * 2 + y_lo), z: 16, core: 2. Of those that a mesh axis runs over, the one named last changes fastest.
Arguments:
- residual: float32 [4, 64, 2, 320, 128], P('row', 'sector', 'band'), may hold values from -8 to 8
- block_inverse: float32 [4, 64, 2, 320, 320], P('row', 'sector', 'band'), may hold values from -0.3125 to 0.3125
- cycle_coupling: float32 [4, 64, 320, 320], P('row', 'sector'), as said below
- outlet_flux: float32 [4, 64, 2, 80, 320], P('row', 'sector', 'band'), may hold values from -0.3125 to 0.3125
- inlet_lift: float32 [4, 64, 2, 320, 80], P('row', 'sector', 'band'), may hold values from -0.5 to 0.5
- mortar_shift: int32 [3], replicated, may hold values from 0 to 63
Outputs:
- correction: float32 [4, 64, 2, 320, 128], P('row', 'sector', 'band')
- outlet_traces: float32 [4, 64, 2, 80, 128], P('row', 'sector', 'band')
The draws below stay inside these ranges and needn't reach their ends.
Inputs may be any that keep to these rules, and one draw needn't show every extreme that they name: `mortar_shift`: one sector shift for each of the 3 interfaces between consecutive rows. `cycle_coupling`: each matrix is a positive diagonal plus full off-diagonal entries.
All inputs are finite; a program needn't handle non-finite values.
Results may differ from the reference program's by a relative error of at most 0.00017.
Values sent between devices are 32-bit elements; how exact they have to be, the bound alone decides.
No kernel may reach another device: no remote copies, remote signals or barrier semaphores. Data moves between devices by JAX's collectives and lax.ppermute only.
A program may use at most 64 MiB of HBM per device.

```python
import jax
import jax.numpy as jnp
from jax import lax

BLK = 320
FACE = 80
LB = 128
BLADE_ROWS = 4
SECTOR_COUNT = 64
BANDS = 2


def draw_cycle_coupling(key, part):
    random_keys = jax.random.split(jax.random.fold_in(key, 7), 6)
    slow_share = 0.5
    spread = 0.2
    slow_part = jax.random.uniform(random_keys[0], (BLADE_ROWS, SECTOR_COUNT, BLK)) < slow_share
    memory = jax.random.uniform(random_keys[1], (BLADE_ROWS, SECTOR_COUNT, BLK), minval=0.3, maxval=1.5)
    fast = jax.random.uniform(random_keys[2], (BLADE_ROWS, SECTOR_COUNT, BLK), minval=0.2, maxval=0.6)
    decay_rate = jnp.where(slow_part, jnp.exp(-memory / SECTOR_COUNT), fast)
    sudden_jump = jax.random.uniform(random_keys[3], (BLADE_ROWS, SECTOR_COUNT, 1)) < 2.0 / SECTOR_COUNT
    sector_split = jax.random.uniform(random_keys[4], (BLADE_ROWS, SECTOR_COUNT, BLK), minval=0.5, maxval=0.8)
    decay_rate = jnp.where(jnp.logical_and(sudden_jump, slow_part), decay_rate * sector_split, decay_rate)
    off_diag = jax.random.normal(random_keys[5], (BLADE_ROWS, SECTOR_COUNT, BLK, BLK), jnp.float32) * (spread / BLK ** 0.5)
    eye = jnp.eye(BLK, dtype=jnp.float32)
    return off_diag + decay_rate[..., None] * eye


def block_scale(stream_key, shape, cuts, low, top_value):
    loudness = 1.0
    for position, blocks in cuts:
        heights = jax.random.uniform(jax.random.fold_in(jax.random.fold_in(stream_key, 6), position), (blocks,), jnp.float32, low / len(cuts), top_value / len(cuts))
        loudness = loudness * jnp.repeat(jnp.exp(heights), shape[position] // blocks).reshape((-1,) + (1,) * (len(shape) - 1 - position))
    return loudness


def scatter_about(own_key, extent, width, bound, shards=(), kind=jnp.bfloat16):
    values = jax.random.normal(own_key, extent, jnp.float32) * width
    if len(shards) > 0:
        values = block_scale(own_key, extent, shards, -0.22, 0.18) * values
    return jnp.clip(values, min=-bound, max=bound).astype(kind)


def setup_inputs(seed: int = 0) -> dict:
    key_list = jax.random.split(jax.random.key(seed), 7)
    residual = scatter_about(key_list[0], (BLADE_ROWS, SECTOR_COUNT, BANDS, BLK, LB), 1.0, 8.0, ((0, 4), (1, 64), (2, 2)), jnp.float32)
    block_inverse = scatter_about(key_list[1], (BLADE_ROWS, SECTOR_COUNT, BANDS, BLK, BLK), BLK ** -0.5, 0.3125, ((0, 4), (1, 64), (2, 2)), jnp.float32)
    cycle_coupling = draw_cycle_coupling(jax.random.fold_in(key_list[6], 71), 0)
    outlet_flux = scatter_about(key_list[3], (BLADE_ROWS, SECTOR_COUNT, BANDS, FACE, BLK), BLK ** -0.5, 0.3125, ((0, 4), (1, 64), (2, 2)), jnp.float32)
    inlet_lift = scatter_about(key_list[4], (BLADE_ROWS, SECTOR_COUNT, BANDS, BLK, FACE), (2 * FACE) ** -0.5, 0.5, ((0, 4), (1, 64), (2, 2)), jnp.float32)
    mortar_shift = jax.random.randint(key_list[5], (BLADE_ROWS - 1,), 0, SECTOR_COUNT).astype(jnp.int32)
    return dict(residual=residual, block_inverse=block_inverse, cycle_coupling=cycle_coupling, outlet_flux=outlet_flux, inlet_lift=inlet_lift, mortar_shift=mortar_shift)


HIGH = lax.Precision.HIGHEST


def cycle_solve(coupling, source):
    eye = jnp.eye(coupling.shape[1], dtype=jnp.float32)
    zero = jnp.zeros(source.shape[1:], jnp.float32)

    def forward(carry, item):
        matrix, state = carry
        link, term = item
        nxt = (jnp.dot(link, matrix, precision=HIGH),
               term + jnp.einsum('ij,bjl->bil', link, state, precision=HIGH))
        return nxt, carry

    def backward(carry, item):
        matrix, state = carry
        link, term = item
        nxt = (jnp.dot(matrix, link, precision=HIGH),
               state + jnp.einsum('ij,bjl->bil', matrix, term, precision=HIGH))
        return nxt, carry

    _, (pre_mat, pre_state) = lax.scan(forward, (eye, zero), (coupling, source))
    _, (suf_mat, suf_state) = lax.scan(backward, (eye, zero), (coupling, source), reverse=True)
    arrive = pre_state + jnp.einsum('sij,sbjl->sbil', pre_mat, suf_state, precision=HIGH)
    return source + jnp.einsum('sij,sbjl->sbil', coupling, arrive, precision=HIGH)


def reference(residual, block_inverse, cycle_coupling, outlet_flux, inlet_lift, mortar_shift):
    source = jnp.einsum('rsbij,rsbjl->rsbil', block_inverse, residual, precision=HIGH)
    solved = lax.map(lambda pair: cycle_solve(pair[0], pair[1]), (cycle_coupling, source))
    rows_out = [solved[0]]
    for section in range(1, BLADE_ROWS):
        trace = jnp.einsum('sbfj,sbjl->sbfl', outlet_flux[section - 1], rows_out[-1], precision=HIGH)
        moved = jnp.roll(trace, mortar_shift[section - 1], axis=0)
        rows_out.append(solved[section] + jnp.einsum('sbjf,sbfl->sbjl', inlet_lift[section], moved, precision=HIGH))
    correction = jnp.stack(rows_out, axis=0)
    outlet_traces = jnp.einsum('rsbfj,rsbjl->rsbfl', outlet_flux, correction, precision=HIGH)
    return correction, outlet_traces
```

```python
import jax
import jax.numpy as jnp
from jax import lax
from jax.sharding import PartitionSpec as P

HIGH = lax.Precision.HIGHEST
FINE = 4


def from_behind(block, axis, distance):
    devices = range(lax.axis_size(axis))
    route = [((i - distance) % len(devices), i) for i in devices]
    return lax.ppermute(block, axis, route)


def apply_block(matrix, state):
    return jnp.einsum("ij,bjl->bil", matrix, state, precision=HIGH)


def hop_down(trace, rows, sectors, step):
    route = [
        (row * sectors + s, (row + 1) * sectors + (s + step) % sectors)
        for row in range(rows - 1)
        for s in range(sectors)
    ]
    return lax.ppermute(trace, ("row", "sector"), route)


def turn(trace, rows, sectors, step):
    if step == 0:
        return trace
    route = [
        (row * sectors + s, row * sectors + (s + step) % sectors)
        for row in range(1, rows)
        for s in range(sectors)
    ]
    return lax.ppermute(trace, ("row", "sector"), route)


def cross(trace, shift, rows, sectors):
    fine = [lambda t, k=k: hop_down(t, rows, sectors, k) for k in range(FINE)]
    coarse = [lambda t, k=k: turn(t, rows, sectors, k) for k in range(0, sectors, FINE)]
    trace = lax.switch(shift % FINE, fine, trace)
    return lax.switch(shift // FINE, coarse, trace)


def on_device(residual, block_inverse, cycle_coupling, outlet_flux, inlet_lift, mortar_shift):
    res_local = residual[0, 0]
    inverse = block_inverse[0, 0]
    coupling = cycle_coupling[0, 0]
    flux = outlet_flux[0, 0, 0]
    lift = inlet_lift[0, 0, 0]
    source = jnp.einsum("bij,bjl->bil", inverse, res_local, precision=HIGH)
    sectors = lax.axis_size("sector")
    levels = sectors.bit_length() - 1
    matrix = coupling
    state = source
    for level in range(levels):
        if level + 1 < levels:
            prev_matrix, prev_state = from_behind((matrix, state), "sector", 2**level)
            state = state + apply_block(matrix, prev_state)
            matrix = jnp.dot(matrix, prev_matrix, precision=HIGH)
        else:
            prev_state = from_behind(state, "sector", 2**level)
            state = state + apply_block(matrix, prev_state)
    state = state[0]
    rows = lax.axis_size("row")
    row_index = lax.axis_index("row")
    shifts = jnp.remainder(mortar_shift, sectors)
    gain = jnp.dot(flux, lift, precision=HIGH)
    base = jnp.dot(flux, state, precision=HIGH)
    trace = base
    inlet = jnp.zeros_like(base)
    for section in range(1, rows):
        moved = cross(trace, shifts[section - 1], rows, sectors)
        inlet = jnp.where(row_index == section, moved, inlet)
        trace = base + jnp.dot(gain, inlet, precision=HIGH)
    current = state + jnp.dot(lift, inlet, precision=HIGH)
    return (current[None, None, None], trace[None, None, None])


def solution(mesh):
    in_specs = (
        P("row", "sector", "band", None, None),
        P("row", "sector", "band", None, None),
        P("row", "sector", None, None),
        P("row", "sector", "band", None, None),
        P("row", "sector", "band", None, None),
        P(),
    )
    out_specs = (P("row", "sector", "band", None, None), P("row", "sector", "band", None, None))
    return jax.shard_map(
        on_device, mesh=mesh, in_specs=in_specs, out_specs=out_specs, check_vma=False
    )
```

```python
import jax
import jax.numpy as jnp
from jax import lax
from jax.experimental import pallas as pl
from jax.experimental.pallas import tpu as pltpu
from jax.sharding import PartitionSpec as P

HIGH = lax.Precision.HIGHEST
FINE = 4
LANES = 128


def dot(a, b):
    return jnp.dot(a, b, precision=HIGH, preferred_element_type=jnp.float32)


def fold(part):
    half = part.shape[0] // 2
    return jnp.concatenate([part[:half], part[half:]], axis=1)


def unfold(part):
    half = part.shape[1] // 2
    return jnp.concatenate([part[:, :half], part[:, half:]], axis=0)


def first_kernel(inverse_ref, residual_ref, coupling_ref, out_ref):
    n = coupling_ref.shape[0]
    out_ref[0:n] = coupling_ref[:, 0:LANES]
    out_ref[n : 2 * n] = coupling_ref[:, LANES : 2 * LANES]
    out_ref[2 * n : 2 * n + n // 2] = fold(coupling_ref[:, 2 * LANES :])
    out_ref[2 * n + n // 2 :] = dot(inverse_ref[...], residual_ref[...])


def window(ref, n):
    return jnp.concatenate(
        [ref[0:n], ref[n : 2 * n], unfold(ref[2 * n : 2 * n + n // 2])], axis=1
    )


def join(late_ref, early_ref, out_ref):
    n = 2 * late_ref.shape[0] // 7
    start = 2 * n + n // 2
    late = window(late_ref, n)
    early = jnp.concatenate(
        [early_ref[0:n], early_ref[n : 2 * n], early_ref[start:], unfold(early_ref[2 * n : start])],
        axis=1,
    )
    both = dot(late, early)
    out_ref[0:n] = both[:, 0:LANES]
    out_ref[n : 2 * n] = both[:, LANES : 2 * LANES]
    out_ref[start:] = late_ref[start:] + both[:, 2 * LANES : 3 * LANES]
    out_ref[2 * n : start] = fold(both[:, 3 * LANES :])


def join_kernel(mirrored_ref, own_ref, got_ref, out_ref):
    mirrored = mirrored_ref[0]

    @pl.when(mirrored == 0)
    def _():
        join(own_ref, got_ref, out_ref)

    @pl.when(mirrored != 0)
    def _():
        join(got_ref, own_ref, out_ref)


def close_kernel(own_ref, got_ref, out_ref):
    n = got_ref.shape[0]
    out_ref[...] = own_ref[2 * n + n // 2 :] + dot(window(own_ref, n), got_ref[...])


VMEM = pl.BlockSpec(memory_space=pltpu.VMEM)
SMEM = pl.BlockSpec(memory_space=pltpu.SMEM)


def call(kernel, specs, shape, *operands):
    return pl.pallas_call(
        kernel,
        out_shape=jax.ShapeDtypeStruct(shape, jnp.float32),
        in_specs=specs,
        out_specs=VMEM,
        compiler_params=pltpu.CompilerParams(vmem_limit_bytes=12 << 20),
    )(*operands)


def sector_route(rows, sectors, step):
    return [
        (row * sectors + s, row * sectors + (s + step(row)) % sectors)
        for row in range(rows)
        if step(row) is not None
        for s in range(sectors)
    ]


def hop_down(trace, rows, sectors, step):
    route = [
        (row * sectors + s, (row + 1) * sectors + (s + step) % sectors)
        for row in range(rows - 1)
        for s in range(sectors)
    ]
    return lax.ppermute(trace, ("row", "sector"), route)


def turn(trace, rows, sectors, step):
    if step == 0:
        return trace
    route = [
        (row * sectors + s, row * sectors + (s + step) % sectors)
        for row in range(1, rows)
        for s in range(sectors)
    ]
    return lax.ppermute(trace, ("row", "sector"), route)


def cross(trace, shift, rows, sectors):
    fine = [lambda t, k=k: hop_down(t, rows, sectors, k) for k in range(FINE)]
    coarse = [lambda t, k=k: turn(t, rows, sectors, k) for k in range(0, sectors, FINE)]
    trace = lax.switch(shift % FINE, fine, trace)
    return lax.switch(shift // FINE, coarse, trace)


def on_device(residual, block_inverse, cycle_coupling, outlet_flux, inlet_lift, mortar_shift):
    flux = outlet_flux[0, 0, 0]
    lift = inlet_lift[0, 0, 0]
    n = cycle_coupling.shape[-1]
    rows = lax.axis_size("row")
    row_index = lax.axis_index("row")
    sectors = lax.axis_size("sector")
    levels = sectors.bit_length() - 1
    axes = ("row", "sector")
    odd = row_index % 2
    mirrored = jnp.reshape(odd, (1,)).astype(jnp.int32)
    shape = (3 * n + n // 2, LANES)

    held = call(
        first_kernel, [VMEM] * 3, shape, block_inverse[0, 0, 0], residual[0, 0, 0], cycle_coupling[0, 0]
    )
    for level in range(levels - 1):
        step = 2**level
        route = sector_route(rows, sectors, lambda row: -step if row % 2 else step)
        got = lax.ppermute(held, axes, route)
        held = call(join_kernel, [SMEM, VMEM, VMEM], shape, mirrored, held, got)
    half = 2 ** (levels - 1)
    route = sector_route(rows, sectors, lambda row: half)
    got = lax.ppermute(held[2 * n + n // 2 :], axes, route)
    state = call(close_kernel, [VMEM] * 2, (n, LANES), held, got)
    route = sector_route(rows, sectors, lambda row: half - 1 if row % 2 else None)
    homed = lax.ppermute(state, axes, route)

    shifts = jnp.remainder(mortar_shift, sectors)
    gain = dot(flux, lift)
    trace = dot(flux, state)
    moved = cross(trace, shifts[0], rows, sectors)
    state = jnp.where(odd == 1, homed, state)
    base = dot(flux, state)
    inlet = jnp.where(row_index == 1, moved, 0.0)
    for section in range(2, rows):
        moved = cross(base + dot(gain, inlet), shifts[section - 1], rows, sectors)
        inlet = jnp.where(row_index == section, moved, inlet)
    current = state + dot(lift, inlet)
    trace = base + dot(gain, inlet)
    return (current[None, None, None], trace[None, None, None])


def solution(mesh):
    in_specs = (
        P("row", "sector", "band", None, None),
        P("row", "sector", "band", None, None),
        P("row", "sector", None, None),
        P("row", "sector", "band", None, None),
        P("row", "sector", "band", None, None),
        P(),
    )
    out_specs = (P("row", "sector", "band", None, None), P("row", "sector", "band", None, None))
    return jax.shard_map(
        on_device, mesh=mesh, in_specs=in_specs, out_specs=out_specs, check_vma=False
    )
```

```python
import functools

import jax
import jax.numpy as jnp
from jax import lax
from jax.experimental import pallas as pl
from jax.experimental.pallas import tpu as pltpu
from jax.sharding import PartitionSpec as P


HIGH = lax.Precision.HIGHEST
FINE = 4
LANES = 128
HEAD = 128


def dot(a, b):
    return jnp.dot(a, b, precision=HIGH, preferred_element_type=jnp.float32)


def fold(part):
    half = part.shape[0] // 2
    return jnp.concatenate([part[:half], part[half:]], axis=1)


def unfold(part):
    half = part.shape[1] // 2
    return jnp.concatenate([part[:, :half], part[:, half:]], axis=0)


def chunk_rows(n):
    tail = n - HEAD
    return max(n + n // 2, HEAD * 7 // 2), max(2 * n, tail * 7 // 2)


def mirrored_parts(ref, h):
    end = 2 * h + h // 2
    return ref[0:h], ref[h : 2 * h], unfold(ref[2 * h : end]), ref[end : end + h]


def put_mirrored(ref, h, parts):
    end = 2 * h + h // 2
    ref[0:h], ref[h : 2 * h], ref[2 * h : end], ref[end : end + h] = (
        parts[0],
        parts[1],
        fold(parts[2]),
        parts[3],
    )
    if end + h < ref.shape[0]:
        ref[end + h :] = jnp.zeros((ref.shape[0] - end - h, LANES), jnp.float32)


def forward_matrix(a_ref, b_ref, n):
    return jnp.concatenate([b_ref[0:n], b_ref[n : 2 * n], unfold(a_ref[n : n + n // 2])], axis=1)


def mirrored_all(a_ref, b_ref, n):
    top, low = mirrored_parts(a_ref, HEAD), mirrored_parts(b_ref, n - HEAD)
    return [jnp.concatenate(pair, axis=0) for pair in zip(top, low)]


def put_forward_a(ref, n, state, last):
    ref[0:n] = state
    ref[n : n + n // 2] = fold(last)


def put_forward_b(ref, n, first, second):
    ref[0:n] = first
    ref[n : 2 * n] = second
    if 2 * n < ref.shape[0]:
        ref[2 * n :] = jnp.zeros((ref.shape[0] - 2 * n, LANES), jnp.float32)


def first_kernel(
    mirrored_ref, inverse_hbm, residual_hbm, coupling_hbm, a_ref, b_ref, inverse, residual, coupling, sems
):
    n = coupling.shape[0]
    copies = [
        pltpu.make_async_copy(source, target, sems.at[i])
        for i, (source, target) in enumerate(
            [(inverse_hbm, inverse), (residual_hbm, residual), (coupling_hbm, coupling)]
        )
    ]
    for copy in copies:
        copy.start()
    for copy in copies:
        copy.wait()
    state = dot(inverse[...], residual[...])

    @pl.when(mirrored_ref[0] == 0)
    def _():
        put_forward_a(a_ref, n, state, coupling[:, 2 * LANES :])
        put_forward_b(b_ref, n, coupling[:, 0:LANES], coupling[:, LANES : 2 * LANES])

    @pl.when(mirrored_ref[0] != 0)
    def _():
        for ref, low, high in ((a_ref, 0, HEAD), (b_ref, HEAD, n)):
            rows = coupling[low:high]
            parts = (rows[:, 0:LANES], rows[:, LANES : 2 * LANES], rows[:, 2 * LANES :], state[low:high])
            put_mirrored(ref, high - low, parts)


def join_mirrored(n, h, a_ref, b_ref, got_ref, out_ref):
    got = mirrored_parts(got_ref, h)
    own = mirrored_all(a_ref, b_ref, n)
    both = dot(
        jnp.concatenate(got[:3], axis=1), jnp.concatenate([own[0], own[1], own[3], own[2]], axis=1)
    )
    state = got[3] + both[:, 2 * LANES : 3 * LANES]
    put_mirrored(
        out_ref, h, (both[:, 0:LANES], both[:, LANES : 2 * LANES], both[:, 3 * LANES :], state)
    )
    return state


def join_a_kernel(n, mirrored_ref, a_ref, b_ref, got_ref, out_ref, head_ref=None):
    @pl.when(mirrored_ref[0] == 0)
    def _():
        matrix = forward_matrix(a_ref, b_ref, n)
        both = dot(matrix, jnp.concatenate([got_ref[0:n], unfold(got_ref[n : n + n // 2])], axis=1))
        state = a_ref[0:n] + both[:, 0:LANES]
        put_forward_a(out_ref, n, state, both[:, LANES:])
        if head_ref is not None:
            head_ref[...] = state[0:HEAD]

    @pl.when(mirrored_ref[0] != 0)
    def _():
        state = join_mirrored(n, HEAD, a_ref, b_ref, got_ref, out_ref)
        if head_ref is not None:
            head_ref[...] = state


def join_b_kernel(n, mirrored_ref, a_ref, b_ref, got_ref, *refs):
    new_a_ref, out_ref, rest_ref = refs if len(refs) == 3 else (None, refs[0], None)

    @pl.when(mirrored_ref[0] == 0)
    def _():
        matrix = forward_matrix(a_ref, b_ref, n)
        both = dot(matrix, jnp.concatenate([got_ref[0:n], got_ref[n : 2 * n]], axis=1))
        put_forward_b(out_ref, n, both[:, 0:LANES], both[:, LANES:])
        if rest_ref is not None:
            rest_ref[...] = new_a_ref[HEAD:n]

    @pl.when(mirrored_ref[0] != 0)
    def _():
        state = join_mirrored(n, n - HEAD, a_ref, b_ref, got_ref, out_ref)
        if rest_ref is not None:
            rest_ref[...] = state


def close_kernel(mirrored_ref, a_ref, b_ref, got_ref, out_ref):
    n = out_ref.shape[0]
    got = got_ref[...]

    @pl.when(mirrored_ref[0] == 0)
    def _():
        out_ref[...] = a_ref[0:n] + dot(forward_matrix(a_ref, b_ref, n), got)

    @pl.when(mirrored_ref[0] != 0)
    def _():
        own = mirrored_all(a_ref, b_ref, n)
        out_ref[...] = own[3] + dot(jnp.concatenate(own[:3], axis=1), got)


VMEM = pl.BlockSpec(memory_space=pltpu.VMEM)
SMEM = pl.BlockSpec(memory_space=pltpu.SMEM)
HBM = pl.BlockSpec(memory_space=pltpu.HBM)


def call(kernel, specs, shapes, *operands, scratch=()):
    shapes = [jax.ShapeDtypeStruct(shape, jnp.float32) for shape in shapes]
    out = pl.pallas_call(
        kernel,
        out_shape=shapes,
        in_specs=specs,
        out_specs=[VMEM] * len(shapes),
        scratch_shapes=scratch,
        compiler_params=pltpu.CompilerParams(vmem_limit_bytes=12 << 20),
    )(*operands)
    return out[0] if len(shapes) == 1 else out


def sector_route(rows, sectors, step):
    return [
        (row * sectors + s, row * sectors + (s + step(row)) % sectors)
        for row in range(rows)
        if step(row) is not None
        for s in range(sectors)
    ]


def is_mirrored(row):
    return (row + 1) // 2 % 2 == 0


def hop(trace, shift, senders, sectors):
    def send(step, trace):
        route = [
            (row * sectors + s, (row + 1) * sectors + (s + step) % sectors)
            for row in senders
            for s in range(sectors)
        ]
        return lax.ppermute(trace, ("row", "sector"), route)

    return lax.switch(shift % FINE, [functools.partial(send, k) for k in range(FINE)], trace)


def turn(trace, shift, rows, sectors):
    def send(step, trace):
        if step == 0:
            return trace
        route = sector_route(rows, sectors, lambda row: step if row else None)
        return lax.ppermute(trace, ("row", "sector"), route)

    steps = [functools.partial(send, k) for k in range(0, sectors, FINE)]
    return lax.switch(shift // FINE, steps, trace)


def on_device(residual, block_inverse, cycle_coupling, outlet_flux, inlet_lift, mortar_shift):
    flux = outlet_flux[0, 0, 0]
    lift = inlet_lift[0, 0, 0]
    n = cycle_coupling.shape[-1]
    rows = lax.axis_size("row")
    row_index = lax.axis_index("row")
    sectors = lax.axis_size("sector")
    last = sectors.bit_length() - 2
    half = sectors // 2
    axes = ("row", "sector")
    mirror = is_mirrored(row_index)
    mirrored = jnp.reshape(mirror, (1,)).astype(jnp.int32)
    rows_a, rows_b = [(count, LANES) for count in chunk_rows(n)]

    def move(block, step):
        route = sector_route(rows, sectors, lambda row: -step if is_mirrored(row) else step)
        return lax.ppermute(block, axes, route)

    a, b = call(
        first_kernel,
        [SMEM, HBM, HBM, HBM],
        [rows_a, rows_b],
        mirrored,
        block_inverse[0, 0, 0],
        residual[0, 0, 0],
        cycle_coupling[0, 0],
        scratch=[
            pltpu.VMEM((n, n), jnp.float32),
            pltpu.VMEM((n, LANES), jnp.float32),
            pltpu.VMEM((n, n), jnp.float32),
            pltpu.SemaphoreType.DMA((3,)),
        ],
    )
    join_a = functools.partial(join_a_kernel, n)
    join_b = functools.partial(join_b_kernel, n)

    def step_a(level, *blocks):
        shapes = [rows_a] if level < last else [rows_a, (HEAD, LANES)]
        return call(join_a, [SMEM] + [VMEM] * 3, shapes, mirrored, *blocks)

    def step_b(level, *blocks):
        shapes = [rows_b] if level < last else [rows_b, (n - HEAD, LANES)]
        return call(join_b, [SMEM] + [VMEM] * len(blocks), shapes, mirrored, *blocks)

    got_a = move(a, 1)
    got_b = move(b, 1)
    for level in range(1, last):
        new_a = step_a(level, a, b, got_a)
        next_a = move(new_a, 2**level)
        got_b = lax.optimization_barrier((got_b, new_a))[0]
        new_b = step_b(level, a, b, got_b)
        if level == 1:
            early = lax.optimization_barrier((flux, new_b))[0]
            route = sector_route(rows, sectors, lambda row: None if row else 1 - half)
            early = lax.ppermute(early, axes, route)
        if level == 2:
            new_b, early = lax.optimization_barrier((new_b, early))
        next_b = move(new_b, 2**level)
        a, b, got_a, got_b = new_a, new_b, next_a, next_b
    new_a, top = step_a(last, a, b, got_a)
    got_b = lax.optimization_barrier((got_b, new_a))[0]
    new_b, low = step_b(last, a, b, got_b, new_a)
    window = jnp.concatenate([top, low], axis=0)
    got = lax.ppermute(window, axes, sector_route(rows, sectors, lambda row: half))
    state = call(close_kernel, [SMEM] + [VMEM] * 3, [(n, LANES)], mirrored, new_a, new_b, got)

    shifts = jnp.remainder(mortar_shift, sectors)
    gain = dot(flux, lift)
    base = dot(jnp.where(row_index == 0, early, flux), state)
    inlet = jnp.zeros_like(base)
    for section in range(1, rows):
        leaving = base + dot(gain, inlet) if section > 1 else base
        shift = shifts[section - 1]
        senders = [0] if section == 1 else range(1, rows - 1)
        if section == 1:
            shift = (shift + half - 1) % sectors
        moved = hop(leaving, shift, senders, sectors)
        if section == 1:
            going, moved = lax.optimization_barrier((state, moved))
            route = sector_route(rows, sectors, lambda row: half - 1 if is_mirrored(row) else None)
            homed = lax.ppermute(going, axes, route)
            moved = jnp.where(shift >= 0, moved, 0.0)
        moved = turn(moved, shift, rows, sectors)
        inlet = jnp.where(row_index == section, moved, inlet)
    state = jnp.where(mirror, homed, state)
    current = state + dot(lift, inlet)
    trace = dot(flux, state) + dot(gain, inlet)
    return (current[None, None, None], trace[None, None, None])


def solution(mesh):
    in_specs = (
        P("row", "sector", "band", None, None),
        P("row", "sector", "band", None, None),
        P("row", "sector", None, None),
        P("row", "sector", "band", None, None),
        P("row", "sector", "band", None, None),
        P(),
    )
    out_specs = (P("row", "sector", "band", None, None), P("row", "sector", "band", None, None))

    return jax.shard_map(
        on_device, mesh=mesh, in_specs=in_specs, out_specs=out_specs, check_vma=False
    )
```

```python
import functools

import jax
import jax.numpy as jnp
from jax import lax
from jax.experimental import pallas as pl
from jax.experimental.pallas import tpu as pltpu
from jax.sharding import PartitionSpec as P


HIGH = lax.Precision.HIGHEST
FINE = 4
LANES = 128
HEAD = 128


def dot(a, b):
    return jnp.dot(a, b, precision=HIGH, preferred_element_type=jnp.float32)


def fold(part):
    half = part.shape[0] // 2
    return jnp.concatenate([part[:half], part[half:]], axis=1)


def unfold(part):
    half = part.shape[1] // 2
    return jnp.concatenate([part[:, :half], part[:, half:]], axis=0)


def chunk_rows(n):
    tail = n - HEAD
    return max(n + n // 2, HEAD * 7 // 2), max(2 * n, tail * 7 // 2)


def mirrored_parts(ref, h):
    end = 2 * h + h // 2
    return ref[0:h], ref[h : 2 * h], unfold(ref[2 * h : end]), ref[end : end + h]


def put_mirrored(ref, h, parts):
    end = 2 * h + h // 2
    ref[0:h], ref[h : 2 * h], ref[2 * h : end], ref[end : end + h] = (
        parts[0],
        parts[1],
        fold(parts[2]),
        parts[3],
    )
    if end + h < ref.shape[0]:
        ref[end + h :] = jnp.zeros((ref.shape[0] - end - h, LANES), jnp.float32)


def forward_matrix(a_ref, b_ref, n):
    return jnp.concatenate([b_ref[0:n], b_ref[n : 2 * n], unfold(a_ref[n : n + n // 2])], axis=1)


def mirrored_all(a_ref, b_ref, n):
    top, low = mirrored_parts(a_ref, HEAD), mirrored_parts(b_ref, n - HEAD)
    return [jnp.concatenate(pair, axis=0) for pair in zip(top, low)]


def put_forward_a(ref, n, state, last):
    ref[0:n] = state
    ref[n : n + n // 2] = fold(last)


def put_forward_b(ref, n, first, second):
    ref[0:n] = first
    ref[n : 2 * n] = second
    if 2 * n < ref.shape[0]:
        ref[2 * n :] = jnp.zeros((ref.shape[0] - 2 * n, LANES), jnp.float32)


def first_kernel(
    mirrored_ref, inverse_hbm, residual_hbm, coupling_hbm, a_ref, b_ref, inverse, residual, coupling, sems
):
    n = coupling.shape[0]
    copies = [
        pltpu.make_async_copy(source, target, sems.at[i])
        for i, (source, target) in enumerate(
            [(inverse_hbm, inverse), (residual_hbm, residual), (coupling_hbm, coupling)]
        )
    ]
    for copy in copies:
        copy.start()
    for copy in copies:
        copy.wait()
    state = dot(inverse[...], residual[...])

    @pl.when(mirrored_ref[0] == 0)
    def _():
        put_forward_a(a_ref, n, state, coupling[:, 2 * LANES :])
        put_forward_b(b_ref, n, coupling[:, 0:LANES], coupling[:, LANES : 2 * LANES])

    @pl.when(mirrored_ref[0] != 0)
    def _():
        for ref, low, high in ((a_ref, 0, HEAD), (b_ref, HEAD, n)):
            rows = coupling[low:high]
            parts = (rows[:, 0:LANES], rows[:, LANES : 2 * LANES], rows[:, 2 * LANES :], state[low:high])
            put_mirrored(ref, high - low, parts)


def join_mirrored(n, h, a_ref, b_ref, got_ref, out_ref):
    got = mirrored_parts(got_ref, h)
    own = mirrored_all(a_ref, b_ref, n)
    both = dot(
        jnp.concatenate(got[:3], axis=1), jnp.concatenate([own[0], own[1], own[3], own[2]], axis=1)
    )
    state = got[3] + both[:, 2 * LANES : 3 * LANES]
    put_mirrored(
        out_ref, h, (both[:, 0:LANES], both[:, LANES : 2 * LANES], both[:, 3 * LANES :], state)
    )
    return state


def join_a_kernel(n, mirrored_ref, a_ref, b_ref, got_ref, out_ref, head_ref=None):
    @pl.when(mirrored_ref[0] == 0)
    def _():
        matrix = forward_matrix(a_ref, b_ref, n)
        both = dot(matrix, jnp.concatenate([got_ref[0:n], unfold(got_ref[n : n + n // 2])], axis=1))
        state = a_ref[0:n] + both[:, 0:LANES]
        put_forward_a(out_ref, n, state, both[:, LANES:])
        if head_ref is not None:
            head_ref[...] = state[0:HEAD]

    @pl.when(mirrored_ref[0] != 0)
    def _():
        state = join_mirrored(n, HEAD, a_ref, b_ref, got_ref, out_ref)
        if head_ref is not None:
            head_ref[...] = state


def join_b_kernel(n, mirrored_ref, a_ref, b_ref, got_ref, *refs):
    new_a_ref, out_ref, rest_ref = refs if len(refs) == 3 else (None, refs[0], None)

    @pl.when(mirrored_ref[0] == 0)
    def _():
        matrix = forward_matrix(a_ref, b_ref, n)
        both = dot(matrix, jnp.concatenate([got_ref[0:n], got_ref[n : 2 * n]], axis=1))
        put_forward_b(out_ref, n, both[:, 0:LANES], both[:, LANES:])
        if rest_ref is not None:
            rest_ref[...] = new_a_ref[HEAD:n]

    @pl.when(mirrored_ref[0] != 0)
    def _():
        state = join_mirrored(n, n - HEAD, a_ref, b_ref, got_ref, out_ref)
        if rest_ref is not None:
            rest_ref[...] = state


def close_kernel(mirrored_ref, a_ref, b_ref, got_ref, out_ref):
    n = out_ref.shape[0]
    got = got_ref[...]

    @pl.when(mirrored_ref[0] == 0)
    def _():
        out_ref[...] = a_ref[0:n] + dot(forward_matrix(a_ref, b_ref, n), got)

    @pl.when(mirrored_ref[0] != 0)
    def _():
        own = mirrored_all(a_ref, b_ref, n)
        out_ref[...] = own[3] + dot(jnp.concatenate(own[:3], axis=1), got)


VMEM = pl.BlockSpec(memory_space=pltpu.VMEM)
SMEM = pl.BlockSpec(memory_space=pltpu.SMEM)
HBM = pl.BlockSpec(memory_space=pltpu.HBM)


def call(kernel, specs, shapes, *operands, scratch=()):
    shapes = [jax.ShapeDtypeStruct(shape, jnp.float32) for shape in shapes]
    out = pl.pallas_call(
        kernel,
        out_shape=shapes,
        in_specs=specs,
        out_specs=[VMEM] * len(shapes),
        scratch_shapes=scratch,
        compiler_params=pltpu.CompilerParams(vmem_limit_bytes=12 << 20),
    )(*operands)
    return out[0] if len(shapes) == 1 else out


def sector_route(rows, sectors, step):
    return [
        (row * sectors + s, row * sectors + (s + step(row)) % sectors)
        for row in range(rows)
        if step(row) is not None
        for s in range(sectors)
    ]


def is_mirrored(row):
    return (row + 1) // 2 % 2 == 0


def hop(trace, shift, senders, sectors):
    def send(step, trace):
        route = [
            (row * sectors + s, (row + 1) * sectors + (s + step) % sectors)
            for row in senders
            for s in range(sectors)
        ]
        return lax.ppermute(trace, ("row", "sector"), route)

    return lax.switch(shift % FINE, [functools.partial(send, k) for k in range(FINE)], trace)


def turn(trace, shift, rows, sectors):
    def send(step, trace):
        if step == 0:
            return trace
        route = sector_route(rows, sectors, lambda row: step if row else None)
        return lax.ppermute(trace, ("row", "sector"), route)

    steps = [functools.partial(send, k) for k in range(0, sectors, FINE)]
    return lax.switch(shift // FINE, steps, trace)


def on_device(residual, block_inverse, cycle_coupling, outlet_flux, inlet_lift, mortar_shift):
    flux = outlet_flux[0, 0, 0]
    lift = inlet_lift[0, 0, 0]
    n = cycle_coupling.shape[-1]
    rows = lax.axis_size("row")
    row_index = lax.axis_index("row")
    sectors = lax.axis_size("sector")
    last = sectors.bit_length() - 2
    half = sectors // 2
    axes = ("row", "sector")
    mirror = is_mirrored(row_index)
    mirrored = jnp.reshape(mirror, (1,)).astype(jnp.int32)
    rows_a, rows_b = [(count, LANES) for count in chunk_rows(n)]

    def move(block, step):
        route = sector_route(rows, sectors, lambda row: -step if is_mirrored(row) else step)
        return lax.ppermute(block, axes, route)

    a, b = call(
        first_kernel,
        [SMEM, HBM, HBM, HBM],
        [rows_a, rows_b],
        mirrored,
        *[
            pltpu.with_memory_space_constraint(block, pltpu.HBM)
            for block in (block_inverse[0, 0, 0], residual[0, 0, 0], cycle_coupling[0, 0])
        ],
        scratch=[
            pltpu.VMEM((n, n), jnp.float32),
            pltpu.VMEM((n, LANES), jnp.float32),
            pltpu.VMEM((n, n), jnp.float32),
            pltpu.SemaphoreType.DMA((3,)),
        ],
    )
    join_a = functools.partial(join_a_kernel, n)
    join_b = functools.partial(join_b_kernel, n)

    def step_a(level, *blocks):
        shapes = [rows_a] if level < last else [rows_a, (HEAD, LANES)]
        return call(join_a, [SMEM] + [VMEM] * 3, shapes, mirrored, *blocks)

    def step_b(level, *blocks):
        shapes = [rows_b] if level < last else [rows_b, (n - HEAD, LANES)]
        return call(join_b, [SMEM] + [VMEM] * len(blocks), shapes, mirrored, *blocks)

    got_a = move(a, 1)
    got_b = move(b, 1)
    early = lax.ppermute(
        flux, axes, sector_route(rows, sectors, lambda row: None if row else 1 - half)
    )
    for level in range(1, last):
        new_a = step_a(level, a, b, got_a)
        next_a = move(new_a, 2**level)
        got_b = lax.optimization_barrier((got_b, new_a))[0]
        new_b = step_b(level, a, b, got_b)
        next_b = move(new_b, 2**level)
        a, b, got_a, got_b = new_a, new_b, next_a, next_b
    new_a, top = step_a(last, a, b, got_a)
    got_b = lax.optimization_barrier((got_b, new_a))[0]
    new_b, low = step_b(last, a, b, got_b, new_a)
    window = jnp.concatenate([top, low], axis=0)
    got = lax.ppermute(window, axes, sector_route(rows, sectors, lambda row: half))
    state = call(close_kernel, [SMEM] + [VMEM] * 3, [(n, LANES)], mirrored, new_a, new_b, got)

    shifts = jnp.remainder(mortar_shift, sectors)
    gain = dot(flux, lift)
    base = dot(jnp.where(row_index == 0, early, flux), state)
    inlet = jnp.zeros_like(base)
    for section in range(1, rows):
        leaving = base + dot(gain, inlet) if section > 1 else base
        shift = shifts[section - 1]
        senders = [0] if section == 1 else range(1, rows - 1)
        if section == 1:
            shift = (shift + half - 1) % sectors
        moved = hop(leaving, shift, senders, sectors)
        if section == 1:
            going, moved = lax.optimization_barrier((state, moved))
            route = sector_route(rows, sectors, lambda row: half - 1 if is_mirrored(row) else None)
            homed = lax.ppermute(going, axes, route)
            moved = jnp.where(shift >= 0, moved, 0.0)
        moved = turn(moved, shift, rows, sectors)
        inlet = jnp.where(row_index == section, moved, inlet)
    state = jnp.where(mirror, homed, state)
    current = state + dot(lift, inlet)
    trace = dot(flux, state) + dot(gain, inlet)
    return (current[None, None, None], trace[None, None, None])


def solution(mesh):
    in_specs = (
        P("row", "sector", "band", None, None),
        P("row", "sector", "band", None, None),
        P("row", "sector", None, None),
        P("row", "sector", "band", None, None),
        P("row", "sector", "band", None, None),
        P(),
    )
    out_specs = (P("row", "sector", "band", None, None), P("row", "sector", "band", None, None))

    return jax.shard_map(
        on_device, mesh=mesh, in_specs=in_specs, out_specs=out_specs, check_vma=False
    )
```

```python
import functools

import jax
import jax.numpy as jnp
from jax import lax
from jax.experimental import pallas as pl
from jax.experimental.pallas import tpu as pltpu
from jax.sharding import PartitionSpec as P


HIGH = lax.Precision.HIGHEST
FINE = 4
LANES = 128
HEAD = 128


def dot(a, b):
    return jnp.dot(a, b, precision=HIGH, preferred_element_type=jnp.float32)


def fold(part):
    half = part.shape[0] // 2
    return jnp.concatenate([part[:half], part[half:]], axis=1)


def unfold(part):
    half = part.shape[1] // 2
    return jnp.concatenate([part[:, :half], part[:, half:]], axis=0)


def chunk_rows(n):
    tail = n - HEAD
    return max(n + n // 2, HEAD * 7 // 2), max(2 * n, tail * 7 // 2)


def mirrored_parts(ref, h):
    end = 2 * h + h // 2
    return ref[0:h], ref[h : 2 * h], unfold(ref[2 * h : end]), ref[end : end + h]


def put_mirrored(ref, h, parts):
    end = 2 * h + h // 2
    ref[0:h], ref[h : 2 * h], ref[2 * h : end], ref[end : end + h] = (
        parts[0],
        parts[1],
        fold(parts[2]),
        parts[3],
    )
    if end + h < ref.shape[0]:
        ref[end + h :] = jnp.zeros((ref.shape[0] - end - h, LANES), jnp.float32)


def forward_matrix(a_ref, b_ref, n):
    return jnp.concatenate([b_ref[0:n], b_ref[n : 2 * n], unfold(a_ref[n : n + n // 2])], axis=1)


def mirrored_all(a_ref, b_ref, n):
    top, low = mirrored_parts(a_ref, HEAD), mirrored_parts(b_ref, n - HEAD)
    return [jnp.concatenate(pair, axis=0) for pair in zip(top, low)]


def put_forward_a(ref, n, state, last):
    ref[0:n] = state
    ref[n : n + n // 2] = fold(last)


def put_forward_b(ref, n, first, second):
    ref[0:n] = first
    ref[n : 2 * n] = second
    if 2 * n < ref.shape[0]:
        ref[2 * n :] = jnp.zeros((ref.shape[0] - 2 * n, LANES), jnp.float32)


def first_kernel(
    mirrored_ref, inverse_hbm, residual_hbm, coupling_hbm, a_ref, b_ref, inverse, residual, coupling, sems
):
    n = coupling.shape[0]
    copies = [
        pltpu.make_async_copy(source, target, sems.at[i])
        for i, (source, target) in enumerate(
            [(inverse_hbm, inverse), (residual_hbm, residual), (coupling_hbm, coupling)]
        )
    ]
    for copy in copies:
        copy.start()
    for copy in copies:
        copy.wait()
    state = dot(inverse[...], residual[...])

    @pl.when(mirrored_ref[0] == 0)
    def _():
        put_forward_a(a_ref, n, state, coupling[:, 2 * LANES :])
        put_forward_b(b_ref, n, coupling[:, 0:LANES], coupling[:, LANES : 2 * LANES])

    @pl.when(mirrored_ref[0] != 0)
    def _():
        for ref, low, high in ((a_ref, 0, HEAD), (b_ref, HEAD, n)):
            rows = coupling[low:high]
            parts = (rows[:, 0:LANES], rows[:, LANES : 2 * LANES], rows[:, 2 * LANES :], state[low:high])
            put_mirrored(ref, high - low, parts)


def join_mirrored(n, h, a_ref, b_ref, got_ref, out_ref):
    got = mirrored_parts(got_ref, h)
    own = mirrored_all(a_ref, b_ref, n)
    both = dot(
        jnp.concatenate(got[:3], axis=1), jnp.concatenate([own[0], own[1], own[3], own[2]], axis=1)
    )
    state = got[3] + both[:, 2 * LANES : 3 * LANES]
    put_mirrored(
        out_ref, h, (both[:, 0:LANES], both[:, LANES : 2 * LANES], both[:, 3 * LANES :], state)
    )
    return state


def join_a_kernel(n, mirrored_ref, a_ref, b_ref, got_ref, out_ref):
    @pl.when(mirrored_ref[0] == 0)
    def _():
        matrix = forward_matrix(a_ref, b_ref, n)
        both = dot(matrix, jnp.concatenate([got_ref[0:n], unfold(got_ref[n : n + n // 2])], axis=1))
        put_forward_a(out_ref, n, a_ref[0:n] + both[:, 0:LANES], both[:, LANES:])

    @pl.when(mirrored_ref[0] != 0)
    def _():
        join_mirrored(n, HEAD, a_ref, b_ref, got_ref, out_ref)


def join_b_kernel(n, mirrored_ref, a_ref, b_ref, got_ref, out_ref):
    @pl.when(mirrored_ref[0] == 0)
    def _():
        matrix = forward_matrix(a_ref, b_ref, n)
        both = dot(matrix, jnp.concatenate([got_ref[0:n], got_ref[n : 2 * n]], axis=1))
        put_forward_b(out_ref, n, both[:, 0:LANES], both[:, LANES:])

    @pl.when(mirrored_ref[0] != 0)
    def _():
        join_mirrored(n, n - HEAD, a_ref, b_ref, got_ref, out_ref)


def split_kernel(n, mirrored_ref, band_ref, a_ref, b_ref, got_ref, new_a_ref, m_ref, s_ref, half_ref):
    m = n + n // 2

    @pl.when(mirrored_ref[0] == 0)
    def _():
        matrix = forward_matrix(a_ref, b_ref, n)
        both = dot(matrix, jnp.concatenate([got_ref[0:n], got_ref[n : 2 * n]], axis=1))
        m_ref[0:n] = both[:, 0:LANES]
        m_ref[n : 2 * n] = both[:, LANES:]
        m_ref[2 * n :] = new_a_ref[n:m]
        s_ref[...] = new_a_ref[0:n]

    @pl.when(mirrored_ref[0] != 0)
    def _():
        got = mirrored_parts(got_ref, n - HEAD)
        own = mirrored_all(a_ref, b_ref, n)
        both = dot(
            jnp.concatenate(got[:3], axis=1), jnp.concatenate([own[0], own[1], own[3], own[2]], axis=1)
        )
        top = mirrored_parts(new_a_ref, HEAD)
        m_ref[0:HEAD] = top[0]
        m_ref[HEAD:n] = both[:, 0:LANES]
        m_ref[n : n + HEAD] = top[1]
        m_ref[n + HEAD : 2 * n] = both[:, LANES : 2 * LANES]
        m_ref[2 * n :] = fold(jnp.concatenate([top[2], both[:, 3 * LANES :]], axis=0))
        s_ref[0:HEAD] = top[3]
        s_ref[HEAD:n] = got[3] + both[:, 2 * LANES : 3 * LANES]

    count = half_ref.shape[0]
    half_ref[...] = m_ref[pl.ds(pl.multiple_of(band_ref[0] * count, 8), count)]


def whole(ref, n):
    return jnp.concatenate([ref[0:n], ref[n : 2 * n], unfold(ref[2 * n :])], axis=1)


def put_halves(band_ref, mine_ref, other_ref, both_ref):
    count = mine_ref.shape[0]
    both_ref[pl.ds(pl.multiple_of(band_ref[0] * count, 8), count)] = mine_ref[...]
    both_ref[pl.ds(pl.multiple_of((1 - band_ref[0]) * count, 8), count)] = other_ref[...]


def state_kernel(mirrored_ref, band_ref, m_ref, s_ref, mine_ref, other_ref, got_ref, out_ref, gotm_ref):
    n = s_ref.shape[0]
    put_halves(band_ref, mine_ref, other_ref, gotm_ref)

    @pl.when(mirrored_ref[0] == 0)
    def _():
        out_ref[...] = s_ref[...] + dot(whole(m_ref, n), got_ref[...])

    @pl.when(mirrored_ref[0] != 0)
    def _():
        out_ref[...] = got_ref[...] + dot(whole(gotm_ref, n), s_ref[...])


def square_kernel(mirrored_ref, m_ref, gotm_ref, out_ref):
    n = out_ref.shape[0]

    @pl.when(mirrored_ref[0] == 0)
    def _():
        out_ref[...] = dot(whole(m_ref, n), whole(gotm_ref, n))

    @pl.when(mirrored_ref[0] != 0)
    def _():
        out_ref[...] = dot(whole(gotm_ref, n), whole(m_ref, n))


def close_kernel(m_ref, s_ref, got_ref, out_ref):
    out_ref[...] = s_ref[...] + dot(m_ref[...], got_ref[...])


VMEM = pl.BlockSpec(memory_space=pltpu.VMEM)
SMEM = pl.BlockSpec(memory_space=pltpu.SMEM)
HBM = pl.BlockSpec(memory_space=pltpu.HBM)


def call(kernel, specs, shapes, *operands, scratch=()):
    shapes = [jax.ShapeDtypeStruct(shape, jnp.float32) for shape in shapes]
    out = pl.pallas_call(
        kernel,
        out_shape=shapes,
        in_specs=specs,
        out_specs=[VMEM] * len(shapes),
        scratch_shapes=scratch,
        compiler_params=pltpu.CompilerParams(vmem_limit_bytes=12 << 20),
    )(*operands)
    return out[0] if len(shapes) == 1 else out


def sector_route(rows, sectors, step):
    return [
        (row * sectors + s, row * sectors + (s + step(row)) % sectors)
        for row in range(rows)
        if step(row) is not None
        for s in range(sectors)
    ]


def is_mirrored(row):
    return (row + 1) // 2 % 2 == 0


def hop(trace, shift, senders, sectors):
    def send(step, trace):
        route = [
            (row * sectors + s, (row + 1) * sectors + (s + step) % sectors)
            for row in senders
            for s in range(sectors)
        ]
        return lax.ppermute(trace, ("row", "sector"), route)

    return lax.switch(shift & (FINE - 1), [functools.partial(send, k) for k in range(FINE)], trace)


def turn(trace, shift, rows, sectors):
    def send(step, trace):
        if step == 0:
            return trace
        first = 0 if step == sectors // 2 else 1
        route = sector_route(rows, sectors, lambda row: step if row >= first else None)
        return lax.ppermute(trace, ("row", "sector"), route)

    steps = [functools.partial(send, k) for k in range(0, sectors, FINE)]
    return lax.switch(shift >> 2, steps, trace)


def on_device(residual, block_inverse, cycle_coupling, outlet_flux, inlet_lift, mortar_shift):
    flux = outlet_flux[0, 0, 0]
    lift = inlet_lift[0, 0, 0]
    n = cycle_coupling.shape[-1]
    rows = lax.axis_size("row")
    row_index = lax.axis_index("row")
    sectors = lax.axis_size("sector")
    last = sectors.bit_length() - 2
    half = sectors // 2
    axes = ("row", "sector")
    mirror = is_mirrored(row_index)
    mirrored = jnp.reshape(mirror, (1,)).astype(jnp.int32)
    rows_a, rows_b = [(count, LANES) for count in chunk_rows(n)]

    def move(block, step):
        route = sector_route(rows, sectors, lambda row: -step if is_mirrored(row) else step)
        return lax.ppermute(block, axes, route)

    a, b = call(
        first_kernel,
        [SMEM, HBM, HBM, HBM],
        [rows_a, rows_b],
        mirrored,
        *[
            pltpu.with_memory_space_constraint(block, pltpu.HBM)
            for block in (block_inverse[0, 0, 0], residual[0, 0, 0], cycle_coupling[0, 0])
        ],
        scratch=[
            pltpu.VMEM((n, n), jnp.float32),
            pltpu.VMEM((n, LANES), jnp.float32),
            pltpu.VMEM((n, n), jnp.float32),
            pltpu.SemaphoreType.DMA((3,)),
        ],
    )
    join_a = functools.partial(join_a_kernel, n)
    join_b = functools.partial(join_b_kernel, n)

    def step(kernel, shapes, *blocks):
        return call(kernel, [SMEM] + [VMEM] * len(blocks), shapes, mirrored, *blocks)

    got_a = move(a, 1)
    got_b = move(b, 1)
    early = lax.ppermute(
        flux, axes, sector_route(rows, sectors, lambda row: None if row else 1 - half)
    )
    for level in range(1, last - 1):
        new_a = step(join_a, [rows_a], a, b, got_a)
        next_a = move(new_a, 2**level)
        got_b = lax.optimization_barrier((got_b, new_a))[0]
        new_b = step(join_b, [rows_b], a, b, got_b)
        next_b = move(new_b, 2**level)
        a, b, got_a, got_b = new_a, new_b, next_a, next_b

    new_a = step(join_a, [rows_a], a, b, got_a)
    got_b = lax.optimization_barrier((got_b, new_a))[0]
    count = n + n // 4
    band = jnp.reshape(lax.axis_index("band"), (1,)).astype(jnp.int32)
    matrix, state, mine = call(
        functools.partial(split_kernel, n),
        [SMEM] * 2 + [VMEM] * 4,
        [(2 * count, LANES), (n, LANES), (count, LANES)],
        mirrored,
        band,
        a,
        b,
        got_b,
        new_a,
    )
    got_mine = move(mine, half // 2)
    got = move(state, half // 2)
    got_other = lax.ppermute(got_mine, "band", [(0, 1), (1, 0)])
    state, got_matrix = call(
        state_kernel,
        [SMEM] * 2 + [VMEM] * 5,
        [(n, LANES), (2 * count, LANES)],
        mirrored,
        band,
        matrix,
        state,
        got_mine,
        got_other,
        got,
    )
    got = lax.ppermute(state, axes, sector_route(rows, sectors, lambda row: half))
    matrix = step(square_kernel, [(n, n)], matrix, got_matrix)
    state = call(close_kernel, [VMEM] * 3, [(n, LANES)], matrix, state, got)

    shifts = mortar_shift & (sectors - 1)
    gain = dot(flux, lift)
    base = dot(jnp.where(row_index == 0, early, flux), state)
    inlet = jnp.zeros_like(base)
    for section in range(1, rows):
        leaving = base + dot(gain, inlet) if section > 1 else base
        shift = shifts[section - 1]
        senders = [0] if section == 1 else range(1, rows - 1)
        if section == 1:
            shift = (shift + half - 1) & (sectors - 1)
        moved = hop(leaving, shift, senders, sectors)
        if section == 1:
            going, moved = lax.optimization_barrier((state, moved))
            route = sector_route(rows, sectors, lambda row: half - 1 if is_mirrored(row) else None)
            homed = lax.ppermute(going, axes, route)
            moved = jnp.where(shift >= 0, moved, 0.0)
        moved = turn(moved, shift, rows, sectors)
        inlet = jnp.where(row_index == section, moved, inlet)
    state = jnp.where(mirror, homed, state)
    current = state + dot(lift, inlet)
    trace = dot(flux, state) + dot(gain, inlet)
    return (current[None, None, None], trace[None, None, None])


def solution(mesh):
    in_specs = (
        P("row", "sector", "band", None, None),
        P("row", "sector", "band", None, None),
        P("row", "sector", None, None),
        P("row", "sector", "band", None, None),
        P("row", "sector", "band", None, None),
        P(),
    )
    out_specs = (P("row", "sector", "band", None, None), P("row", "sector", "band", None, None))

    return jax.shard_map(
        on_device, mesh=mesh, in_specs=in_specs, out_specs=out_specs, check_vma=False
    )
```

```python
import functools

import jax
import jax.numpy as jnp
from jax import lax
from jax.experimental import pallas as pl
from jax.experimental.pallas import tpu as pltpu
from jax.sharding import PartitionSpec as P


HIGH = lax.Precision.HIGHEST
FINE = 4
LANES = 128
HEAD = 128


def dot(a, b):
    return jnp.dot(a, b, precision=HIGH, preferred_element_type=jnp.float32)


def fold(part):
    half = part.shape[0] // 2
    return jnp.concatenate([part[:half], part[half:]], axis=1)


def unfold(part):
    half = part.shape[1] // 2
    return jnp.concatenate([part[:, :half], part[:, half:]], axis=0)


def chunk_rows(n):
    tail = n - HEAD
    return max(n + n // 2, HEAD * 7 // 2), max(2 * n, tail * 7 // 2)


def chunks(ref, n):
    count = chunk_rows(n)[0]
    return ref.at[0:count], ref.at[count:]


def mirrored_parts(ref, h):
    end = 2 * h + h // 2
    return ref[0:h], ref[h : 2 * h], unfold(ref[2 * h : end]), ref[end : end + h]


def put_mirrored(ref, h, parts):
    end = 2 * h + h // 2
    ref[0:h], ref[h : 2 * h], ref[2 * h : end], ref[end : end + h] = (
        parts[0],
        parts[1],
        fold(parts[2]),
        parts[3],
    )
    if end + h < ref.shape[0]:
        ref[end + h :] = jnp.zeros((ref.shape[0] - end - h, LANES), jnp.float32)


def forward_matrix(a_ref, b_ref, n):
    return jnp.concatenate([b_ref[0:n], b_ref[n : 2 * n], unfold(a_ref[n : n + n // 2])], axis=1)


def mirrored_all(a_ref, b_ref, n):
    top, low = mirrored_parts(a_ref, HEAD), mirrored_parts(b_ref, n - HEAD)
    return [jnp.concatenate(pair, axis=0) for pair in zip(top, low)]


def put_forward_a(ref, n, state, last):
    ref[0:n] = state
    ref[n : n + n // 2] = fold(last)


def put_forward_b(ref, n, first, second):
    ref[0:n] = first
    ref[n : 2 * n] = second
    if 2 * n < ref.shape[0]:
        ref[2 * n :] = jnp.zeros((ref.shape[0] - 2 * n, LANES), jnp.float32)


def first_kernel(
    mirrored_ref, inverse_hbm, residual_hbm, coupling_hbm, both_ref, inverse, residual, coupling, sems
):
    n = coupling.shape[0]
    a_ref, b_ref = chunks(both_ref, n)
    copies = [
        pltpu.make_async_copy(source, target, sems.at[i])
        for i, (source, target) in enumerate(
            [(inverse_hbm, inverse), (residual_hbm, residual), (coupling_hbm, coupling)]
        )
    ]
    for copy in copies:
        copy.start()
    for copy in copies:
        copy.wait()
    state = dot(inverse[...], residual[...])

    @pl.when(mirrored_ref[0] == 0)
    def _():
        put_forward_a(a_ref, n, state, coupling[:, 2 * LANES :])
        put_forward_b(b_ref, n, coupling[:, 0:LANES], coupling[:, LANES : 2 * LANES])

    @pl.when(mirrored_ref[0] != 0)
    def _():
        for ref, low, high in ((a_ref, 0, HEAD), (b_ref, HEAD, n)):
            rows = coupling[low:high]
            parts = (rows[:, 0:LANES], rows[:, LANES : 2 * LANES], rows[:, 2 * LANES :], state[low:high])
            put_mirrored(ref, high - low, parts)


def join_mirrored(n, h, a_ref, b_ref, got_ref, out_ref):
    got = mirrored_parts(got_ref, h)
    own = mirrored_all(a_ref, b_ref, n)
    both = dot(
        jnp.concatenate(got[:3], axis=1), jnp.concatenate([own[0], own[1], own[3], own[2]], axis=1)
    )
    state = got[3] + both[:, 2 * LANES : 3 * LANES]
    put_mirrored(
        out_ref, h, (both[:, 0:LANES], both[:, LANES : 2 * LANES], both[:, 3 * LANES :], state)
    )
    return state


def join_a_kernel(n, mirrored_ref, a_ref, b_ref, got_ref, out_ref):
    @pl.when(mirrored_ref[0] == 0)
    def _():
        matrix = forward_matrix(a_ref, b_ref, n)
        both = dot(matrix, jnp.concatenate([got_ref[0:n], unfold(got_ref[n : n + n // 2])], axis=1))
        put_forward_a(out_ref, n, a_ref[0:n] + both[:, 0:LANES], both[:, LANES:])

    @pl.when(mirrored_ref[0] != 0)
    def _():
        join_mirrored(n, HEAD, a_ref, b_ref, got_ref, out_ref)


def join_b_kernel(n, mirrored_ref, a_ref, b_ref, got_ref, out_ref):
    @pl.when(mirrored_ref[0] == 0)
    def _():
        matrix = forward_matrix(a_ref, b_ref, n)
        both = dot(matrix, jnp.concatenate([got_ref[0:n], got_ref[n : 2 * n]], axis=1))
        put_forward_b(out_ref, n, both[:, 0:LANES], both[:, LANES:])

    @pl.when(mirrored_ref[0] != 0)
    def _():
        join_mirrored(n, n - HEAD, a_ref, b_ref, got_ref, out_ref)


def first_join_a_kernel(n, mirrored_ref, both_ref, got_ref, out_ref):
    join_a_kernel(n, mirrored_ref, *chunks(both_ref, n), chunks(got_ref, n)[0], out_ref)


def first_join_b_kernel(n, mirrored_ref, both_ref, got_ref, out_ref):
    join_b_kernel(n, mirrored_ref, *chunks(both_ref, n), chunks(got_ref, n)[1], out_ref)


def split_kernel(n, mirrored_ref, band_ref, a_ref, b_ref, got_ref, new_a_ref, m_ref, s_ref, half_ref):
    m = n + n // 2

    @pl.when(mirrored_ref[0] == 0)
    def _():
        matrix = forward_matrix(a_ref, b_ref, n)
        both = dot(matrix, jnp.concatenate([got_ref[0:n], got_ref[n : 2 * n]], axis=1))
        m_ref[0:n] = both[:, 0:LANES]
        m_ref[n : 2 * n] = both[:, LANES:]
        m_ref[2 * n :] = new_a_ref[n:m]
        s_ref[...] = new_a_ref[0:n]

    @pl.when(mirrored_ref[0] != 0)
    def _():
        got = mirrored_parts(got_ref, n - HEAD)
        own = mirrored_all(a_ref, b_ref, n)
        both = dot(
            jnp.concatenate(got[:3], axis=1), jnp.concatenate([own[0], own[1], own[3], own[2]], axis=1)
        )
        top = mirrored_parts(new_a_ref, HEAD)
        m_ref[0:HEAD] = top[0]
        m_ref[HEAD:n] = both[:, 0:LANES]
        m_ref[n : n + HEAD] = top[1]
        m_ref[n + HEAD : 2 * n] = both[:, LANES : 2 * LANES]
        m_ref[2 * n :] = fold(jnp.concatenate([top[2], both[:, 3 * LANES :]], axis=0))
        s_ref[0:HEAD] = top[3]
        s_ref[HEAD:n] = got[3] + both[:, 2 * LANES : 3 * LANES]

    count = half_ref.shape[0]
    half_ref[...] = m_ref[pl.ds(pl.multiple_of(band_ref[0] * count, 8), count)]


def whole(ref, n):
    return jnp.concatenate([ref[0:n], ref[n : 2 * n], unfold(ref[2 * n :])], axis=1)


def put_halves(band_ref, mine_ref, other_ref, both_ref):
    count = mine_ref.shape[0]
    both_ref[pl.ds(pl.multiple_of(band_ref[0] * count, 8), count)] = mine_ref[...]
    both_ref[pl.ds(pl.multiple_of((1 - band_ref[0]) * count, 8), count)] = other_ref[...]


def forward_kernel(m_ref, s_ref, got_ref, out_ref):
    out_ref[...] = s_ref[...] + dot(whole(m_ref, s_ref.shape[0]), got_ref[...])


def mirrored_kernel(band_ref, s_ref, mine_ref, other_ref, got_ref, out_ref, gotm_ref):
    put_halves(band_ref, mine_ref, other_ref, gotm_ref)
    out_ref[...] = got_ref[...] + dot(whole(gotm_ref, s_ref.shape[0]), s_ref[...])


def square_kernel(mirrored_ref, m_ref, gotm_ref, out_ref):
    n = out_ref.shape[0]

    @pl.when(mirrored_ref[0] == 0)
    def _():
        out_ref[...] = dot(whole(m_ref, n), whole(gotm_ref, n))

    @pl.when(mirrored_ref[0] != 0)
    def _():
        out_ref[...] = dot(whole(gotm_ref, n), whole(m_ref, n))


def close_kernel(m_ref, s_ref, got_ref, out_ref):
    out_ref[...] = s_ref[...] + dot(m_ref[...], got_ref[...])


VMEM = pl.BlockSpec(memory_space=pltpu.VMEM)
SMEM = pl.BlockSpec(memory_space=pltpu.SMEM)
HBM = pl.BlockSpec(memory_space=pltpu.HBM)


def call(kernel, specs, shapes, *operands, scratch=()):
    shapes = [jax.ShapeDtypeStruct(shape, jnp.float32) for shape in shapes]
    out = pl.pallas_call(
        kernel,
        out_shape=shapes,
        in_specs=specs,
        out_specs=[VMEM] * len(shapes),
        scratch_shapes=scratch,
        compiler_params=pltpu.CompilerParams(vmem_limit_bytes=12 << 20),
    )(*operands)
    return out[0] if len(shapes) == 1 else out


def sector_route(rows, sectors, step):
    return [
        (row * sectors + s, row * sectors + (s + step(row)) % sectors)
        for row in range(rows)
        if step(row) is not None
        for s in range(sectors)
    ]


def is_mirrored(row):
    return row % 2 == 1


def hop(trace, shift, senders, sectors):
    def send(step, trace):
        route = [
            (row * sectors + s, (row + 1) * sectors + (s + step) % sectors)
            for row in senders
            for s in range(sectors)
        ]
        return lax.ppermute(trace, ("row", "sector"), route)

    return lax.switch(shift & (FINE - 1), [functools.partial(send, k) for k in range(FINE)], trace)


def turn(trace, shift, rows, sectors):
    def send(step, trace):
        if step == 0:
            return trace
        route = sector_route(rows, sectors, lambda row: None if is_mirrored(row) else step)
        return lax.ppermute(trace, ("row", "sector"), route)

    steps = [functools.partial(send, k) for k in range(0, sectors, FINE)]
    return lax.switch(shift >> 2, steps, trace)


def on_device(residual, block_inverse, cycle_coupling, outlet_flux, inlet_lift, mortar_shift):
    flux = outlet_flux[0, 0, 0]
    lift = inlet_lift[0, 0, 0]
    n = cycle_coupling.shape[-1]
    rows = lax.axis_size("row")
    row_index = lax.axis_index("row")
    sectors = lax.axis_size("sector")
    last = sectors.bit_length() - 2
    half = sectors // 2
    axes = ("row", "sector")
    mirror = is_mirrored(row_index)
    mirrored = jnp.reshape(mirror, (1,)).astype(jnp.int32)
    rows_a, rows_b = [(count, LANES) for count in chunk_rows(n)]

    def move(block, step):
        route = sector_route(rows, sectors, lambda row: -step if is_mirrored(row) else step)
        return lax.ppermute(block, axes, route)

    start = call(
        first_kernel,
        [SMEM, HBM, HBM, HBM],
        [(rows_a[0] + rows_b[0], LANES)],
        mirrored,
        *[
            pltpu.with_memory_space_constraint(block, pltpu.HBM)
            for block in (block_inverse[0, 0, 0], residual[0, 0, 0], cycle_coupling[0, 0])
        ],
        scratch=[
            pltpu.VMEM((n, n), jnp.float32),
            pltpu.VMEM((n, LANES), jnp.float32),
            pltpu.VMEM((n, n), jnp.float32),
            pltpu.SemaphoreType.DMA((3,)),
        ],
    )
    join_a = functools.partial(join_a_kernel, n)
    join_b = functools.partial(join_b_kernel, n)

    def step(kernel, shapes, *blocks):
        return call(kernel, [SMEM] + [VMEM] * len(blocks), shapes, mirrored, *blocks)

    got = move(start, 1)
    gain = dot(flux, lift)
    early = lax.ppermute(
        jnp.concatenate([flux, gain], axis=1),
        axes,
        sector_route(rows, sectors, lambda row: 1 - half if row == 1 else None),
    )
    a = step(functools.partial(first_join_a_kernel, n), [rows_a], start, got)
    got_a = move(a, 2)
    b = step(functools.partial(first_join_b_kernel, n), [rows_b], start, got)
    got_b = move(b, 2)
    for level in range(2, last - 1):
        new_a = step(join_a, [rows_a], a, b, got_a)
        next_a = move(new_a, 2**level)
        got_b = lax.optimization_barrier((got_b, new_a))[0]
        new_b = step(join_b, [rows_b], a, b, got_b)
        next_b = move(new_b, 2**level)
        a, b, got_a, got_b = new_a, new_b, next_a, next_b

    new_a = step(join_a, [rows_a], a, b, got_a)
    got_b = lax.optimization_barrier((got_b, new_a))[0]
    count = n + n // 4
    band = jnp.reshape(lax.axis_index("band"), (1,)).astype(jnp.int32)
    matrix, state, mine = call(
        functools.partial(split_kernel, n),
        [SMEM] * 2 + [VMEM] * 4,
        [(2 * count, LANES), (n, LANES), (count, LANES)],
        mirrored,
        band,
        a,
        b,
        got_b,
        new_a,
    )
    got = move(state, half // 2)
    got_mine = move(mine, half // 2)
    ahead = call(forward_kernel, [VMEM] * 3, [(n, LANES)], matrix, state, got)
    route = sector_route(rows, sectors, lambda row: None if is_mirrored(row) else half)
    got_ahead = lax.ppermute(ahead, axes, route)
    got_other = lax.ppermute(got_mine, "band", [(0, 1), (1, 0)])
    behind, got_matrix = call(
        mirrored_kernel,
        [SMEM] + [VMEM] * 4,
        [(n, LANES), (2 * count, LANES)],
        band,
        state,
        got_mine,
        got_other,
        got,
    )
    route = sector_route(rows, sectors, lambda row: half if is_mirrored(row) else None)
    got_behind = lax.ppermute(behind, axes, route)
    matrix = step(square_kernel, [(n, n)], matrix, got_matrix)

    mask = sectors - 1
    state = call(close_kernel, [VMEM] * 3, [(n, LANES)], matrix, ahead, got_ahead)
    shift = (mortar_shift[0] - (half - 1)) & mask
    moved = hop(turn(dot(flux, state), shift, rows, sectors), shift, [0], sectors)
    inlet = jnp.where(row_index == 1, moved, 0.0)

    got_behind = lax.optimization_barrier((got_behind, inlet))[0]
    closed = call(close_kernel, [VMEM] * 3, [(n, LANES)], matrix, behind, got_behind)
    state = jnp.where(mirror, closed, state)
    base = dot(jnp.where(row_index == 1, early[:, :n], flux), state)
    local = jnp.where(row_index == 1, early[:, n:], gain)
    for section in range(2, rows):
        leaving = base + dot(local, inlet)
        shift = mortar_shift[section - 1]
        if section == 2:
            shift = shift + (half - 1)
        shift = shift & mask
        if is_mirrored(section):
            leaving = turn(leaving, shift, rows, sectors)
        moved = hop(leaving, shift, range(1, rows - 1), sectors)
        if section == 2:
            going, moved = lax.optimization_barrier((jnp.concatenate([state, inlet], axis=0), moved))
            route = sector_route(rows, sectors, lambda row: half - 1 if is_mirrored(row) else None)
            homed = lax.ppermute(going, axes, route)
            moved = jnp.where(shift >= 0, moved, 0.0)
        if not is_mirrored(section):
            moved = turn(moved, shift, rows, sectors)
        inlet = jnp.where(row_index == section, moved, inlet)
    state = jnp.where(mirror, homed[:n], state)
    inlet = jnp.where(row_index == 1, homed[n:], inlet)
    current = state + dot(lift, inlet)
    trace = dot(flux, state) + dot(gain, inlet)
    return (current[None, None, None], trace[None, None, None])


def solution(mesh):
    in_specs = (
        P("row", "sector", "band", None, None),
        P("row", "sector", "band", None, None),
        P("row", "sector", None, None),
        P("row", "sector", "band", None, None),
        P("row", "sector", "band", None, None),
        P(),
    )
    out_specs = (P("row", "sector", "band", None, None), P("row", "sector", "band", None, None))

    return jax.shard_map(
        on_device, mesh=mesh, in_specs=in_specs, out_specs=out_specs, check_vma=False
    )
```

```python
import functools

import jax
import jax.numpy as jnp
from jax import lax
from jax.experimental import pallas as pl
from jax.experimental.pallas import tpu as pltpu
from jax.sharding import PartitionSpec as P


HIGH = lax.Precision.HIGHEST
FINE = 4
LANES = 128
HEAD = 128


def dot(a, b, contract=(1, 0)):
    dims = (((contract[0],), (contract[1],)), ((), ()))

    def product(x, y):
        return lax.dot_general(x, y, dims, preferred_element_type=jnp.float32)

    a_high, b_high = a.astype(jnp.bfloat16), b.astype(jnp.bfloat16)
    a_low = (a - a_high.astype(jnp.float32)).astype(jnp.bfloat16)
    b_low = (b - b_high.astype(jnp.float32)).astype(jnp.bfloat16)
    return product(a_high, b_high) + (product(a_high, b_low) + product(a_low, b_high))


def exact_dot(a, b):
    return jnp.dot(a, b, precision=HIGH, preferred_element_type=jnp.float32)


def fold(part):
    half = part.shape[0] // 2
    return jnp.concatenate([part[:half], part[half:]], axis=1)


def unfold(part):
    half = part.shape[1] // 2
    return jnp.concatenate([part[:, :half], part[:, half:]], axis=0)


def chunk_rows(n):
    tail = n - HEAD
    return max(n + n // 2, HEAD * 7 // 2), max(2 * n, tail * 7 // 2)


def chunks(ref, n):
    count = chunk_rows(n)[0]
    return ref.at[0:count], ref.at[count:]


def mirrored_parts(ref, h):
    end = 2 * h + h // 2
    return ref[0:h], ref[h : 2 * h], unfold(ref[2 * h : end]), ref[end : end + h]


def put_mirrored(ref, h, parts):
    end = 2 * h + h // 2
    ref[0:h], ref[h : 2 * h], ref[2 * h : end], ref[end : end + h] = (
        parts[0],
        parts[1],
        fold(parts[2]),
        parts[3],
    )
    if end + h < ref.shape[0]:
        ref[end + h :] = jnp.zeros((ref.shape[0] - end - h, LANES), jnp.float32)


def forward_matrix(a_ref, b_ref, n):
    return jnp.concatenate([b_ref[0:n], b_ref[n : 2 * n], unfold(a_ref[n : n + n // 2])], axis=1)


def mirrored_all(a_ref, b_ref, n):
    top, low = mirrored_parts(a_ref, HEAD), mirrored_parts(b_ref, n - HEAD)
    return [jnp.concatenate(pair, axis=0) for pair in zip(top, low)]


def put_forward_a(ref, n, state, last):
    ref[0:n] = state
    ref[n : n + n // 2] = fold(last)


def put_forward_b(ref, n, first, second):
    ref[0:n] = first
    ref[n : 2 * n] = second
    if 2 * n < ref.shape[0]:
        ref[2 * n :] = jnp.zeros((ref.shape[0] - 2 * n, LANES), jnp.float32)


def first_kernel(
    mirrored_ref, inverse_hbm, residual_hbm, coupling_hbm, both_ref, inverse, residual, coupling, sems
):
    n = coupling.shape[0]
    a_ref, b_ref = chunks(both_ref, n)
    copies = [
        pltpu.make_async_copy(source, target, sems.at[i])
        for i, (source, target) in enumerate(
            [(inverse_hbm, inverse), (residual_hbm, residual), (coupling_hbm, coupling)]
        )
    ]
    for copy in copies:
        copy.start()
    for copy in copies:
        copy.wait()
    state = dot(inverse[...], residual[...])

    @pl.when(mirrored_ref[0] == 0)
    def _():
        put_forward_a(a_ref, n, state, coupling[:, 2 * LANES :])
        put_forward_b(b_ref, n, coupling[:, 0:LANES], coupling[:, LANES : 2 * LANES])

    @pl.when(mirrored_ref[0] != 0)
    def _():
        for ref, low, high in ((a_ref, 0, HEAD), (b_ref, HEAD, n)):
            rows = coupling[low:high]
            parts = (rows[:, 0:LANES], rows[:, LANES : 2 * LANES], rows[:, 2 * LANES :], state[low:high])
            put_mirrored(ref, high - low, parts)


def join_mirrored(n, h, a_ref, b_ref, got_ref, out_ref):
    got = mirrored_parts(got_ref, h)
    own = mirrored_all(a_ref, b_ref, n)
    both = dot(
        jnp.concatenate(got[:3], axis=1), jnp.concatenate([own[0], own[1], own[3], own[2]], axis=1)
    )
    state = got[3] + both[:, 2 * LANES : 3 * LANES]
    put_mirrored(
        out_ref, h, (both[:, 0:LANES], both[:, LANES : 2 * LANES], both[:, 3 * LANES :], state)
    )
    return state


def join_a_kernel(n, mirrored_ref, a_ref, b_ref, got_ref, out_ref):
    @pl.when(mirrored_ref[0] == 0)
    def _():
        matrix = forward_matrix(a_ref, b_ref, n)
        both = dot(matrix, jnp.concatenate([got_ref[0:n], unfold(got_ref[n : n + n // 2])], axis=1))
        put_forward_a(out_ref, n, a_ref[0:n] + both[:, 0:LANES], both[:, LANES:])

    @pl.when(mirrored_ref[0] != 0)
    def _():
        join_mirrored(n, HEAD, a_ref, b_ref, got_ref, out_ref)


def join_b_kernel(n, mirrored_ref, a_ref, b_ref, got_ref, out_ref):
    @pl.when(mirrored_ref[0] == 0)
    def _():
        matrix = forward_matrix(a_ref, b_ref, n)
        both = dot(matrix, jnp.concatenate([got_ref[0:n], got_ref[n : 2 * n]], axis=1))
        put_forward_b(out_ref, n, both[:, 0:LANES], both[:, LANES:])

    @pl.when(mirrored_ref[0] != 0)
    def _():
        join_mirrored(n, n - HEAD, a_ref, b_ref, got_ref, out_ref)


def first_join_a_kernel(n, mirrored_ref, both_ref, got_ref, out_ref):
    join_a_kernel(n, mirrored_ref, *chunks(both_ref, n), chunks(got_ref, n)[0], out_ref)


def first_join_b_kernel(n, mirrored_ref, both_ref, got_ref, out_ref):
    join_b_kernel(n, mirrored_ref, *chunks(both_ref, n), chunks(got_ref, n)[1], out_ref)


def split_kernel(n, mirrored_ref, band_ref, a_ref, b_ref, got_ref, new_a_ref, m_ref, s_ref, half_ref):
    m = n + n // 2

    @pl.when(mirrored_ref[0] == 0)
    def _():
        matrix = forward_matrix(a_ref, b_ref, n)
        both = dot(matrix, jnp.concatenate([got_ref[0:n], got_ref[n : 2 * n]], axis=1))
        m_ref[0:n] = both[:, 0:LANES]
        m_ref[n : 2 * n] = both[:, LANES:]
        m_ref[2 * n :] = new_a_ref[n:m]
        s_ref[...] = new_a_ref[0:n]

    @pl.when(mirrored_ref[0] != 0)
    def _():
        got = mirrored_parts(got_ref, n - HEAD)
        own = mirrored_all(a_ref, b_ref, n)
        both = dot(
            jnp.concatenate(got[:3], axis=1), jnp.concatenate([own[0], own[1], own[3], own[2]], axis=1)
        )
        top = mirrored_parts(new_a_ref, HEAD)
        m_ref[0:HEAD] = top[0]
        m_ref[HEAD:n] = both[:, 0:LANES]
        m_ref[n : n + HEAD] = top[1]
        m_ref[n + HEAD : 2 * n] = both[:, LANES : 2 * LANES]
        m_ref[2 * n :] = fold(jnp.concatenate([top[2], both[:, 3 * LANES :]], axis=0))
        s_ref[0:HEAD] = top[3]
        s_ref[HEAD:n] = got[3] + both[:, 2 * LANES : 3 * LANES]

    count = half_ref.shape[0]
    half_ref[...] = m_ref[pl.ds(pl.multiple_of(band_ref[0] * count, 8), count)]


def whole(ref, n):
    return jnp.concatenate([ref[0:n], ref[n : 2 * n], unfold(ref[2 * n :])], axis=1)


def put_halves(band_ref, mine_ref, other_ref, both_ref):
    count = mine_ref.shape[0]
    both_ref[pl.ds(pl.multiple_of(band_ref[0] * count, 8), count)] = mine_ref[...]
    both_ref[pl.ds(pl.multiple_of((1 - band_ref[0]) * count, 8), count)] = other_ref[...]


def forward_kernel(m_ref, s_ref, got_ref, out_ref):
    out_ref[...] = s_ref[...] + dot(whole(m_ref, s_ref.shape[0]), got_ref[...])


def mirrored_kernel(band_ref, s_ref, mine_ref, other_ref, got_ref, out_ref, gotm_ref):
    put_halves(band_ref, mine_ref, other_ref, gotm_ref)
    out_ref[...] = got_ref[...] + dot(whole(gotm_ref, s_ref.shape[0]), s_ref[...])


def square_kernel(mirrored_ref, m_ref, gotm_ref, out_ref):
    n = out_ref.shape[0]

    @pl.when(mirrored_ref[0] == 0)
    def _():
        out_ref[...] = dot(whole(m_ref, n), whole(gotm_ref, n))

    @pl.when(mirrored_ref[0] != 0)
    def _():
        out_ref[...] = dot(whole(gotm_ref, n), whole(m_ref, n))


def close_kernel(m_ref, s_ref, got_ref, out_ref):
    out_ref[...] = s_ref[...] + dot(m_ref[...], got_ref[...])


def second_kernel(
    row_ref, m_ref, s_ref, got_ref, ready_ref, moved_ref, early_ref, flux_ref, gain_ref, going_ref, base_ref, out_ref
):
    n = ready_ref.shape[0]
    mirror = row_ref[0] % 2 == 1

    @pl.when(mirror)
    def _():
        going_ref[0:n] = s_ref[...] + dot(m_ref[...], got_ref[...])

    @pl.when(jnp.logical_not(mirror))
    def _():
        going_ref[0:n] = ready_ref[...]

    @pl.when(row_ref[0] == 1)
    def _():
        going_ref[n:] = moved_ref[...]
        base = dot(early_ref[:, 0:n], going_ref[0:n])
        base_ref[...] = base
        out_ref[...] = base + dot(early_ref[:, n:], moved_ref[...])

    @pl.when(row_ref[0] != 1)
    def _():
        going_ref[n:] = jnp.zeros_like(moved_ref)
        base = dot(flux_ref[...], going_ref[0:n])
        base_ref[...] = base
        out_ref[...] = base


def last_kernel(
    row_ref, going_ref, homed_ref, second_ref, third_ref, lift_ref, flux_ref, gain_ref, state_ref, trace_ref, all_ref
):
    n = state_ref.shape[1]
    row = row_ref[0]

    @pl.when(row % 2 == 1)
    def _():
        all_ref[...] = homed_ref[...]

    @pl.when(row % 2 == 0)
    def _():
        all_ref[...] = going_ref[...]

    for section, moved_ref in ((2, second_ref), (3, third_ref)):

        @pl.when(row == section)
        def _(moved_ref=moved_ref):
            all_ref[n:] = moved_ref[...]

    state_ref[0] = all_ref[0:n] + dot(lift_ref[...], all_ref[n:], (0, 0))
    trace_ref[0] = dot(flux_ref[...], all_ref[0:n]) + dot(gain_ref[...], all_ref[n:])


VMEM = pl.BlockSpec(memory_space=pltpu.VMEM)
SMEM = pl.BlockSpec(memory_space=pltpu.SMEM)
HBM = pl.BlockSpec(memory_space=pltpu.HBM)


def call(kernel, specs, shapes, *operands, scratch=()):
    shapes = [jax.ShapeDtypeStruct(shape, jnp.float32) for shape in shapes]
    out = pl.pallas_call(
        kernel,
        out_shape=shapes,
        in_specs=specs,
        out_specs=[VMEM] * len(shapes),
        scratch_shapes=scratch,
        compiler_params=pltpu.CompilerParams(vmem_limit_bytes=12 << 20),
    )(*operands)
    return out[0] if len(shapes) == 1 else out


def sector_route(rows, sectors, step):
    return [
        (row * sectors + s, row * sectors + (s + step(row)) % sectors)
        for row in range(rows)
        if step(row) is not None
        for s in range(sectors)
    ]


def is_mirrored(row):
    return row % 2 == 1


def hop(trace, shift, senders, sectors):
    def send(step, trace):
        route = [
            (row * sectors + s, (row + 1) * sectors + (s + step) % sectors)
            for row in senders
            for s in range(sectors)
        ]
        return lax.ppermute(trace, ("row", "sector"), route)

    return lax.switch(shift & (FINE - 1), [functools.partial(send, k) for k in range(FINE)], trace)


def turn(trace, shift, rows, sectors):
    def send(step, trace):
        if step == 0:
            return trace
        route = sector_route(rows, sectors, lambda row: None if is_mirrored(row) else step)
        return lax.ppermute(trace, ("row", "sector"), route)

    steps = [functools.partial(send, k) for k in range(0, sectors, FINE)]
    return lax.switch(shift >> 2, steps, trace)


def on_device(residual, block_inverse, cycle_coupling, outlet_flux, inlet_lift, mortar_shift):
    flux = outlet_flux[0, 0, 0]
    lift = inlet_lift[0, 0, 0]
    n = cycle_coupling.shape[-1]
    rows = lax.axis_size("row")
    row_index = lax.axis_index("row")
    sectors = lax.axis_size("sector")
    last = sectors.bit_length() - 2
    half = sectors // 2
    axes = ("row", "sector")
    mirror = is_mirrored(row_index)
    mirrored = jnp.reshape(mirror, (1,)).astype(jnp.int32)
    rows_a, rows_b = [(count, LANES) for count in chunk_rows(n)]

    def move(block, step):
        route = sector_route(rows, sectors, lambda row: -step if is_mirrored(row) else step)
        return lax.ppermute(block, axes, route)

    start = call(
        first_kernel,
        [SMEM, HBM, HBM, HBM],
        [(rows_a[0] + rows_b[0], LANES)],
        mirrored,
        *[
            pltpu.with_memory_space_constraint(block, pltpu.HBM)
            for block in (block_inverse[0, 0, 0], residual[0, 0, 0], cycle_coupling[0, 0])
        ],
        scratch=[
            pltpu.VMEM((n, n), jnp.float32),
            pltpu.VMEM((n, LANES), jnp.float32),
            pltpu.VMEM((n, n), jnp.float32),
            pltpu.SemaphoreType.DMA((3,)),
        ],
    )
    join_a = functools.partial(join_a_kernel, n)
    join_b = functools.partial(join_b_kernel, n)

    def step(kernel, shapes, *blocks):
        return call(kernel, [SMEM] + [VMEM] * len(blocks), shapes, mirrored, *blocks)

    got = move(start, 1)
    gain = exact_dot(flux, lift)
    early = lax.ppermute(
        jnp.concatenate([flux, gain], axis=1),
        axes,
        sector_route(rows, sectors, lambda row: 1 - half if row == 1 else None),
    )
    a = step(functools.partial(first_join_a_kernel, n), [rows_a], start, got)
    got_a = move(a, 2)
    b = step(functools.partial(first_join_b_kernel, n), [rows_b], start, got)
    got_b = move(b, 2)
    for level in range(2, last - 1):
        new_a = step(join_a, [rows_a], a, b, got_a)
        next_a = move(new_a, 2**level)
        got_b = lax.optimization_barrier((got_b, new_a))[0]
        new_b = step(join_b, [rows_b], a, b, got_b)
        next_b = move(new_b, 2**level)
        a, b, got_a, got_b = new_a, new_b, next_a, next_b

    new_a = step(join_a, [rows_a], a, b, got_a)
    got_b = lax.optimization_barrier((got_b, new_a))[0]
    count = n + n // 4
    band = jnp.reshape(lax.axis_index("band"), (1,)).astype(jnp.int32)
    matrix, state, mine = call(
        functools.partial(split_kernel, n),
        [SMEM] * 2 + [VMEM] * 4,
        [(2 * count, LANES), (n, LANES), (count, LANES)],
        mirrored,
        band,
        a,
        b,
        got_b,
        new_a,
    )
    got = move(state, half // 2)
    got_mine = move(mine, half // 2)
    ahead = call(forward_kernel, [VMEM] * 3, [(n, LANES)], matrix, state, got)
    route = sector_route(rows, sectors, lambda row: None if is_mirrored(row) else half)
    got_ahead = lax.ppermute(ahead, axes, route)
    got_other = lax.ppermute(got_mine, "band", [(0, 1), (1, 0)])
    behind, got_matrix = call(
        mirrored_kernel,
        [SMEM] + [VMEM] * 4,
        [(n, LANES), (2 * count, LANES)],
        band,
        state,
        got_mine,
        got_other,
        got,
    )
    route = sector_route(rows, sectors, lambda row: half if is_mirrored(row) else None)
    got_behind = lax.ppermute(behind, axes, route)
    matrix = step(square_kernel, [(n, n)], matrix, got_matrix)

    mask = sectors - 1
    state = call(close_kernel, [VMEM] * 3, [(n, LANES)], matrix, ahead, got_ahead)
    shift = (mortar_shift[0] - (half - 1)) & mask
    moved = hop(turn(exact_dot(flux, state), shift, rows, sectors), shift, [0], sectors)

    row = jnp.reshape(row_index, (1,)).astype(jnp.int32)
    face = (flux.shape[0], LANES)
    going, base, leaving = call(
        second_kernel,
        [SMEM] + [VMEM] * 8,
        [(n + face[0], LANES), face, face],
        row,
        matrix,
        behind,
        got_behind,
        state,
        moved,
        early,
        flux,
        gain,
    )
    shift = (mortar_shift[1] + (half - 1)) & mask
    moved = hop(leaving, shift, range(1, rows - 1), sectors)
    going, moved = lax.optimization_barrier((going, moved))
    route = sector_route(rows, sectors, lambda row: half - 1 if is_mirrored(row) else None)
    homed = lax.ppermute(going, axes, route)
    moved = jnp.where(shift >= 0, moved, 0.0)
    second = turn(moved, shift, rows, sectors)
    shift = mortar_shift[2] & mask
    leaving = turn(base + exact_dot(gain, second), shift, rows, sectors)
    third = hop(leaving, shift, range(1, rows - 1), sectors)
    return call(
        last_kernel,
        [SMEM] + [VMEM] * 7,
        [(1, n, LANES), (1,) + face],
        row,
        going,
        homed,
        second,
        third,
        lift.T,
        flux,
        gain,
        scratch=[pltpu.VMEM((n + face[0], LANES), jnp.float32)],
    )


def solution(mesh):
    in_specs = (
        P("row", "sector", "band", None, None),
        P("row", "sector", "band", None, None),
        P("row", "sector", None, None),
        P("row", "sector", "band", None, None),
        P("row", "sector", "band", None, None),
        P(),
    )
    out_specs = (P("row", "sector", "band", None, None), P("row", "sector", "band", None, None))

    def layer(*operands):
        return tuple(block[None, None] for block in on_device(*operands))

    return jax.shard_map(
        layer, mesh=mesh, in_specs=in_specs, out_specs=out_specs, check_vma=False
    )
```

```python
import functools

import jax
import jax.numpy as jnp
from jax import lax
from jax.experimental import pallas as pl
from jax.experimental.pallas import tpu as pltpu
from jax.sharding import PartitionSpec as P


HIGH = lax.Precision.HIGHEST
FINE = 4
LANES = 128
HEAD = 128


def dot(a, b, contract=(1, 0)):
    dims = (((contract[0],), (contract[1],)), ((), ()))

    def product(x, y):
        return lax.dot_general(x, y, dims, preferred_element_type=jnp.float32)

    a_high, b_high = a.astype(jnp.bfloat16), b.astype(jnp.bfloat16)
    a_low = (a - a_high.astype(jnp.float32)).astype(jnp.bfloat16)
    b_low = (b - b_high.astype(jnp.float32)).astype(jnp.bfloat16)
    return product(a_high, b_high) + (product(a_high, b_low) + product(a_low, b_high))


def exact_dot(a, b):
    return jnp.dot(a, b, precision=HIGH, preferred_element_type=jnp.float32)


def fold(part):
    half = part.shape[0] // 2
    return jnp.concatenate([part[:half], part[half:]], axis=1)


def unfold(part):
    half = part.shape[1] // 2
    return jnp.concatenate([part[:, :half], part[:, half:]], axis=0)


def chunk_rows(n):
    tail = n - HEAD
    return max(n + n // 2, HEAD * 7 // 2), max(2 * n, tail * 7 // 2)


def chunks(ref, n):
    count = chunk_rows(n)[0]
    return ref.at[0:count], ref.at[count:]


def mirrored_parts(ref, h):
    end = 2 * h + h // 2
    return ref[0:h], ref[h : 2 * h], unfold(ref[2 * h : end]), ref[end : end + h]


def put_mirrored(ref, h, parts):
    end = 2 * h + h // 2
    ref[0:h], ref[h : 2 * h], ref[2 * h : end], ref[end : end + h] = (
        parts[0],
        parts[1],
        fold(parts[2]),
        parts[3],
    )
    if end + h < ref.shape[0]:
        ref[end + h :] = jnp.zeros((ref.shape[0] - end - h, LANES), jnp.float32)


def forward_matrix(a_ref, b_ref, n):
    return jnp.concatenate([b_ref[0:n], b_ref[n : 2 * n], unfold(a_ref[n : n + n // 2])], axis=1)


def mirrored_all(a_ref, b_ref, n):
    top, low = mirrored_parts(a_ref, HEAD), mirrored_parts(b_ref, n - HEAD)
    return [jnp.concatenate(pair, axis=0) for pair in zip(top, low)]


def put_forward_a(ref, n, state, last):
    ref[0:n] = state
    ref[n : n + n // 2] = fold(last)


def put_forward_b(ref, n, first, second):
    ref[0:n] = first
    ref[n : 2 * n] = second
    if 2 * n < ref.shape[0]:
        ref[2 * n :] = jnp.zeros((ref.shape[0] - 2 * n, LANES), jnp.float32)


def first_kernel(
    mirrored_ref, inverse_hbm, residual_hbm, coupling_hbm, both_ref, inverse, residual, coupling, sems
):
    n = coupling.shape[0]
    a_ref, b_ref = chunks(both_ref, n)
    copies = [
        pltpu.make_async_copy(source, target, sems.at[i])
        for i, (source, target) in enumerate(
            [(inverse_hbm, inverse), (residual_hbm, residual), (coupling_hbm, coupling)]
        )
    ]
    for copy in copies:
        copy.start()
    for copy in copies:
        copy.wait()
    state = dot(inverse[...], residual[...])

    @pl.when(mirrored_ref[0] == 0)
    def _():
        put_forward_a(a_ref, n, state, coupling[:, 2 * LANES :])
        put_forward_b(b_ref, n, coupling[:, 0:LANES], coupling[:, LANES : 2 * LANES])

    @pl.when(mirrored_ref[0] != 0)
    def _():
        for ref, low, high in ((a_ref, 0, HEAD), (b_ref, HEAD, n)):
            rows = coupling[low:high]
            parts = (rows[:, 0:LANES], rows[:, LANES : 2 * LANES], rows[:, 2 * LANES :], state[low:high])
            put_mirrored(ref, high - low, parts)


def join_mirrored(n, h, a_ref, b_ref, got_ref, out_ref):
    got = mirrored_parts(got_ref, h)
    own = mirrored_all(a_ref, b_ref, n)
    both = dot(
        jnp.concatenate(got[:3], axis=1), jnp.concatenate([own[0], own[1], own[3], own[2]], axis=1)
    )
    state = got[3] + both[:, 2 * LANES : 3 * LANES]
    put_mirrored(
        out_ref, h, (both[:, 0:LANES], both[:, LANES : 2 * LANES], both[:, 3 * LANES :], state)
    )
    return state


def join_a_kernel(n, mirrored_ref, a_ref, b_ref, got_ref, out_ref):
    @pl.when(mirrored_ref[0] == 0)
    def _():
        matrix = forward_matrix(a_ref, b_ref, n)
        both = dot(matrix, jnp.concatenate([got_ref[0:n], unfold(got_ref[n : n + n // 2])], axis=1))
        put_forward_a(out_ref, n, a_ref[0:n] + both[:, 0:LANES], both[:, LANES:])

    @pl.when(mirrored_ref[0] != 0)
    def _():
        join_mirrored(n, HEAD, a_ref, b_ref, got_ref, out_ref)


def join_b_kernel(n, mirrored_ref, a_ref, b_ref, got_ref, out_ref):
    @pl.when(mirrored_ref[0] == 0)
    def _():
        matrix = forward_matrix(a_ref, b_ref, n)
        both = dot(matrix, jnp.concatenate([got_ref[0:n], got_ref[n : 2 * n]], axis=1))
        put_forward_b(out_ref, n, both[:, 0:LANES], both[:, LANES:])

    @pl.when(mirrored_ref[0] != 0)
    def _():
        join_mirrored(n, n - HEAD, a_ref, b_ref, got_ref, out_ref)


def first_join_a_kernel(n, mirrored_ref, both_ref, got_ref, out_ref):
    join_a_kernel(n, mirrored_ref, *chunks(both_ref, n), chunks(got_ref, n)[0], out_ref)


def first_join_b_kernel(n, mirrored_ref, both_ref, got_ref, out_ref):
    join_b_kernel(n, mirrored_ref, *chunks(both_ref, n), chunks(got_ref, n)[1], out_ref)


def split_kernel(n, mirrored_ref, band_ref, a_ref, b_ref, got_ref, new_a_ref, m_ref, s_ref, half_ref):
    m = n + n // 2

    @pl.when(mirrored_ref[0] == 0)
    def _():
        matrix = forward_matrix(a_ref, b_ref, n)
        both = dot(matrix, jnp.concatenate([got_ref[0:n], got_ref[n : 2 * n]], axis=1))
        m_ref[0:n] = both[:, 0:LANES]
        m_ref[n : 2 * n] = both[:, LANES:]
        m_ref[2 * n :] = new_a_ref[n:m]
        s_ref[...] = new_a_ref[0:n]

    @pl.when(mirrored_ref[0] != 0)
    def _():
        got = mirrored_parts(got_ref, n - HEAD)
        own = mirrored_all(a_ref, b_ref, n)
        both = dot(
            jnp.concatenate(got[:3], axis=1), jnp.concatenate([own[0], own[1], own[3], own[2]], axis=1)
        )
        top = mirrored_parts(new_a_ref, HEAD)
        m_ref[0:HEAD] = top[0]
        m_ref[HEAD:n] = both[:, 0:LANES]
        m_ref[n : n + HEAD] = top[1]
        m_ref[n + HEAD : 2 * n] = both[:, LANES : 2 * LANES]
        m_ref[2 * n :] = fold(jnp.concatenate([top[2], both[:, 3 * LANES :]], axis=0))
        s_ref[0:HEAD] = top[3]
        s_ref[HEAD:n] = got[3] + both[:, 2 * LANES : 3 * LANES]

    count = half_ref.shape[0]
    half_ref[...] = m_ref[pl.ds(pl.multiple_of(band_ref[0] * count, 8), count)]


def whole(ref, n):
    return jnp.concatenate([ref[0:n], ref[n : 2 * n], unfold(ref[2 * n :])], axis=1)


def put_halves(band_ref, mine_ref, other_ref, both_ref):
    count = mine_ref.shape[0]
    both_ref[pl.ds(pl.multiple_of(band_ref[0] * count, 8), count)] = mine_ref[...]
    both_ref[pl.ds(pl.multiple_of((1 - band_ref[0]) * count, 8), count)] = other_ref[...]


def forward_kernel(m_ref, s_ref, got_ref, out_ref):
    out_ref[...] = s_ref[...] + dot(whole(m_ref, s_ref.shape[0]), got_ref[...])


def mirrored_kernel(band_ref, s_ref, mine_ref, other_ref, got_ref, out_ref, gotm_ref):
    put_halves(band_ref, mine_ref, other_ref, gotm_ref)
    out_ref[...] = got_ref[...] + dot(whole(gotm_ref, s_ref.shape[0]), s_ref[...])


def square_kernel(mirrored_ref, m_ref, gotm_ref, out_ref):
    n = out_ref.shape[0]

    @pl.when(mirrored_ref[0] == 0)
    def _():
        out_ref[...] = dot(whole(m_ref, n), whole(gotm_ref, n))

    @pl.when(mirrored_ref[0] != 0)
    def _():
        out_ref[...] = dot(whole(gotm_ref, n), whole(m_ref, n))


def close_kernel(m_ref, s_ref, got_ref, out_ref):
    out_ref[...] = s_ref[...] + dot(m_ref[...], got_ref[...])


def second_kernel(
    row_ref, m_ref, s_ref, got_ref, ready_ref, moved_ref, early_ref, flux_ref, gain_ref, going_ref, base_ref, out_ref
):
    n = ready_ref.shape[0]
    mirror = row_ref[0] % 2 == 1

    @pl.when(mirror)
    def _():
        going_ref[0:n] = s_ref[...] + dot(m_ref[...], got_ref[...])

    @pl.when(jnp.logical_not(mirror))
    def _():
        going_ref[0:n] = ready_ref[...]

    @pl.when(row_ref[0] == 1)
    def _():
        going_ref[n:] = moved_ref[...]
        base = dot(early_ref[:, 0:n], going_ref[0:n])
        base_ref[...] = base
        out_ref[...] = base + dot(early_ref[:, n:], moved_ref[...])

    @pl.when(row_ref[0] != 1)
    def _():
        going_ref[n:] = jnp.zeros_like(moved_ref)
        base = dot(flux_ref[...], going_ref[0:n])
        base_ref[...] = base
        out_ref[...] = base


def last_kernel(
    row_ref, going_ref, homed_ref, second_ref, third_ref, lift_ref, flux_ref, gain_ref, state_ref, trace_ref, all_ref
):
    n = state_ref.shape[1]
    row = row_ref[0]

    @pl.when(row % 2 == 1)
    def _():
        all_ref[...] = homed_ref[...]

    @pl.when(row % 2 == 0)
    def _():
        all_ref[...] = going_ref[...]

    for section, moved_ref in ((2, second_ref), (3, third_ref)):

        @pl.when(row == section)
        def _(moved_ref=moved_ref):
            all_ref[n:] = moved_ref[...]

    state_ref[0] = all_ref[0:n] + dot(lift_ref[...], all_ref[n:], (0, 0))
    trace_ref[0] = dot(flux_ref[...], all_ref[0:n]) + dot(gain_ref[...], all_ref[n:])


VMEM = pl.BlockSpec(memory_space=pltpu.VMEM)
SMEM = pl.BlockSpec(memory_space=pltpu.SMEM)
HBM = pl.BlockSpec(memory_space=pltpu.HBM)


def call(kernel, specs, shapes, *operands, scratch=()):
    shapes = [jax.ShapeDtypeStruct(shape, jnp.float32) for shape in shapes]
    out = pl.pallas_call(
        kernel,
        out_shape=shapes,
        in_specs=specs,
        out_specs=[VMEM] * len(shapes),
        scratch_shapes=scratch,
        compiler_params=pltpu.CompilerParams(vmem_limit_bytes=12 << 20),
    )(*operands)
    return out[0] if len(shapes) == 1 else out


def sector_route(rows, sectors, step):
    return [
        (row * sectors + s, row * sectors + (s + step(row)) % sectors)
        for row in range(rows)
        if step(row) is not None
        for s in range(sectors)
    ]


def is_mirrored(row):
    return row % 2 == 1


def hop(trace, shift, senders, sectors):
    def send(step, trace):
        route = [
            (row * sectors + s, (row + 1) * sectors + (s + step) % sectors)
            for row in senders
            for s in range(sectors)
        ]
        return lax.ppermute(trace, ("row", "sector"), route)

    return lax.switch(shift & (FINE - 1), [functools.partial(send, k) for k in range(FINE)], trace)


def turn(trace, shift, rows, sectors):
    def send(step, trace):
        if step == 0:
            return trace
        route = sector_route(rows, sectors, lambda row: None if is_mirrored(row) else step)
        return lax.ppermute(trace, ("row", "sector"), route)

    steps = [functools.partial(send, k) for k in range(0, sectors, FINE)]
    return lax.switch(shift >> 2, steps, trace)


def on_device(residual, block_inverse, cycle_coupling, outlet_flux, inlet_lift, mortar_shift):
    flux = outlet_flux[0, 0, 0]
    lift = inlet_lift[0, 0, 0]
    n = cycle_coupling.shape[-1]
    rows = lax.axis_size("row")
    row_index = lax.axis_index("row")
    sectors = lax.axis_size("sector")
    last = sectors.bit_length() - 2
    half = sectors // 2
    axes = ("row", "sector")
    mirror = is_mirrored(row_index)
    mirrored = jnp.reshape(mirror, (1,)).astype(jnp.int32)
    rows_a, rows_b = [(count, LANES) for count in chunk_rows(n)]

    def move(block, step):
        route = sector_route(rows, sectors, lambda row: -step if is_mirrored(row) else step)
        return lax.ppermute(block, axes, route)

    start = call(
        first_kernel,
        [SMEM, HBM, HBM, HBM],
        [(rows_a[0] + rows_b[0], LANES)],
        mirrored,
        *[
            pltpu.with_memory_space_constraint(block, pltpu.HBM)
            for block in (block_inverse[0, 0, 0], residual[0, 0, 0], cycle_coupling[0, 0])
        ],
        scratch=[
            pltpu.VMEM((n, n), jnp.float32),
            pltpu.VMEM((n, LANES), jnp.float32),
            pltpu.VMEM((n, n), jnp.float32),
            pltpu.SemaphoreType.DMA((3,)),
        ],
    )
    join_a = functools.partial(join_a_kernel, n)
    join_b = functools.partial(join_b_kernel, n)

    def step(kernel, shapes, *blocks):
        return call(kernel, [SMEM] + [VMEM] * len(blocks), shapes, mirrored, *blocks)

    got = move(start, 1)
    gain = exact_dot(flux, lift)
    early = lax.ppermute(
        jnp.concatenate([flux, gain], axis=1),
        axes,
        sector_route(rows, sectors, lambda row: 1 - half if row == 1 else None),
    )
    a = step(functools.partial(first_join_a_kernel, n), [rows_a], start, got)
    got_a = move(a, 2)
    b = step(functools.partial(first_join_b_kernel, n), [rows_b], start, got)
    got_b = move(b, 2)
    for level in range(2, last - 1):
        new_a = step(join_a, [rows_a], a, b, got_a)
        next_a = move(new_a, 2**level)
        got_b = lax.optimization_barrier((got_b, new_a))[0]
        new_b = step(join_b, [rows_b], a, b, got_b)
        next_b = move(new_b, 2**level)
        a, b, got_a, got_b = new_a, new_b, next_a, next_b

    new_a = step(join_a, [rows_a], a, b, got_a)
    got_b = lax.optimization_barrier((got_b, new_a))[0]
    count = n + n // 4
    band = jnp.reshape(lax.axis_index("band"), (1,)).astype(jnp.int32)
    matrix, state, mine = call(
        functools.partial(split_kernel, n),
        [SMEM] * 2 + [VMEM] * 4,
        [(2 * count, LANES), (n, LANES), (count, LANES)],
        mirrored,
        band,
        a,
        b,
        got_b,
        new_a,
    )
    got = move(state, half // 2)
    got_mine = move(mine, half // 2)
    ahead = call(forward_kernel, [VMEM] * 3, [(n, LANES)], matrix, state, got)
    route = sector_route(rows, sectors, lambda row: None if is_mirrored(row) else half)
    got_ahead = lax.ppermute(ahead, axes, route)
    got_other = lax.ppermute(got_mine, "band", [(0, 1), (1, 0)])
    behind, got_matrix = call(
        mirrored_kernel,
        [SMEM] + [VMEM] * 4,
        [(n, LANES), (2 * count, LANES)],
        band,
        state,
        got_mine,
        got_other,
        got,
    )
    route = sector_route(rows, sectors, lambda row: half if is_mirrored(row) else None)
    got_behind = lax.ppermute(behind, axes, route)
    matrix = step(square_kernel, [(n, n)], matrix, got_matrix)

    mask = sectors - 1
    state = call(close_kernel, [VMEM] * 3, [(n, LANES)], matrix, ahead, got_ahead)
    shift = (mortar_shift[0] - (half - 1)) & mask
    moved = hop(turn(exact_dot(flux, state), shift, rows, sectors), shift, range(0, rows - 1, 2), sectors)

    row = jnp.reshape(row_index, (1,)).astype(jnp.int32)
    face = (flux.shape[0], LANES)
    going, base, leaving = call(
        second_kernel,
        [SMEM] + [VMEM] * 8,
        [(n + face[0], LANES), face, face],
        row,
        matrix,
        behind,
        got_behind,
        state,
        moved,
        early,
        flux,
        gain,
    )
    shift = (mortar_shift[1] + (half - 1)) & mask
    moved = hop(leaving, shift, range(1, rows - 1, 2), sectors)
    going, moved = lax.optimization_barrier((going, moved))
    route = sector_route(rows, sectors, lambda row: half - 1 if is_mirrored(row) else None)
    homed = lax.ppermute(going, axes, route)
    second = turn(moved, shift, rows, sectors)
    shift = mortar_shift[2] & mask
    leaving = turn(base + exact_dot(gain, second), shift, rows, sectors)
    third = hop(leaving, shift, range(0, rows - 1, 2), sectors)
    return call(
        last_kernel,
        [SMEM] + [VMEM] * 7,
        [(1, n, LANES), (1,) + face],
        row,
        going,
        homed,
        second,
        third,
        lift.T,
        flux,
        gain,
        scratch=[pltpu.VMEM((n + face[0], LANES), jnp.float32)],
    )


def solution(mesh):
    in_specs = (
        P("row", "sector", "band", None, None),
        P("row", "sector", "band", None, None),
        P("row", "sector", None, None),
        P("row", "sector", "band", None, None),
        P("row", "sector", "band", None, None),
        P(),
    )
    out_specs = (P("row", "sector", "band", None, None), P("row", "sector", "band", None, None))

    def layer(*operands):
        return tuple(block[None, None] for block in on_device(*operands))

    return jax.shard_map(
        layer, mesh=mesh, in_specs=in_specs, out_specs=out_specs, check_vma=False
    )
```

```python
import functools

import jax
import jax.numpy as jnp
from jax import lax
from jax.experimental import pallas as pl
from jax.experimental.pallas import tpu as pltpu
from jax.sharding import PartitionSpec as P


HIGH = lax.Precision.HIGHEST
FINE = 4
LANES = 128
HEAD = 128


def dot(a, b, contract=(1, 0)):
    dims = (((contract[0],), (contract[1],)), ((), ()))

    def product(x, y):
        return lax.dot_general(x, y, dims, preferred_element_type=jnp.float32)

    a_high, b_high = a.astype(jnp.bfloat16), b.astype(jnp.bfloat16)
    a_low = (a - a_high.astype(jnp.float32)).astype(jnp.bfloat16)
    b_low = (b - b_high.astype(jnp.float32)).astype(jnp.bfloat16)
    return product(a_high, b_high) + (product(a_high, b_low) + product(a_low, b_high))


def exact_dot(a, b):
    return jnp.dot(a, b, precision=HIGH, preferred_element_type=jnp.float32)


def fold(part):
    half = part.shape[0] // 2
    return jnp.concatenate([part[:half], part[half:]], axis=1)


def unfold(part):
    half = part.shape[1] // 2
    return jnp.concatenate([part[:, :half], part[:, half:]], axis=0)


def chunk_rows(n):
    tail = n - HEAD
    return max(n + n // 2, HEAD * 7 // 2), max(2 * n, tail * 7 // 2)


def chunks(ref, n):
    count = chunk_rows(n)[0]
    return ref.at[0:count], ref.at[count:]


def mirrored_parts(ref, h):
    end = 2 * h + h // 2
    return ref[0:h], ref[h : 2 * h], unfold(ref[2 * h : end]), ref[end : end + h]


def put_mirrored(ref, h, parts):
    end = 2 * h + h // 2
    ref[0:h], ref[h : 2 * h], ref[2 * h : end], ref[end : end + h] = (
        parts[0],
        parts[1],
        fold(parts[2]),
        parts[3],
    )
    if end + h < ref.shape[0]:
        ref[end + h :] = jnp.zeros((ref.shape[0] - end - h, LANES), jnp.float32)


def forward_matrix(a_ref, b_ref, n):
    return jnp.concatenate([b_ref[0:n], b_ref[n : 2 * n], unfold(a_ref[n : n + n // 2])], axis=1)


def mirrored_all(a_ref, b_ref, n):
    top, low = mirrored_parts(a_ref, HEAD), mirrored_parts(b_ref, n - HEAD)
    return [jnp.concatenate(pair, axis=0) for pair in zip(top, low)]


def put_forward_a(ref, n, state, last):
    ref[0:n] = state
    ref[n : n + n // 2] = fold(last)


def put_forward_b(ref, n, first, second):
    ref[0:n] = first
    ref[n : 2 * n] = second
    if 2 * n < ref.shape[0]:
        ref[2 * n :] = jnp.zeros((ref.shape[0] - 2 * n, LANES), jnp.float32)


def first_kernel(
    mirrored_ref, inverse_hbm, residual_hbm, coupling_hbm, both_ref, inverse, residual, coupling, sems
):
    n = coupling.shape[0]
    a_ref, b_ref = chunks(both_ref, n)
    copies = [
        pltpu.make_async_copy(source, target, sems.at[i])
        for i, (source, target) in enumerate(
            [(inverse_hbm, inverse), (residual_hbm, residual), (coupling_hbm, coupling)]
        )
    ]
    for copy in copies:
        copy.start()
    for copy in copies:
        copy.wait()
    state = dot(inverse[...], residual[...])

    @pl.when(mirrored_ref[0] == 0)
    def _():
        put_forward_a(a_ref, n, state, coupling[:, 2 * LANES :])
        put_forward_b(b_ref, n, coupling[:, 0:LANES], coupling[:, LANES : 2 * LANES])

    @pl.when(mirrored_ref[0] != 0)
    def _():
        for ref, low, high in ((a_ref, 0, HEAD), (b_ref, HEAD, n)):
            rows = coupling[low:high]
            parts = (rows[:, 0:LANES], rows[:, LANES : 2 * LANES], rows[:, 2 * LANES :], state[low:high])
            put_mirrored(ref, high - low, parts)


def join_mirrored(n, h, a_ref, b_ref, got_ref, out_ref):
    got = mirrored_parts(got_ref, h)
    own = mirrored_all(a_ref, b_ref, n)
    both = dot(
        jnp.concatenate(got[:3], axis=1), jnp.concatenate([own[0], own[1], own[3], own[2]], axis=1)
    )
    state = got[3] + both[:, 2 * LANES : 3 * LANES]
    put_mirrored(
        out_ref, h, (both[:, 0:LANES], both[:, LANES : 2 * LANES], both[:, 3 * LANES :], state)
    )
    return state


def join_a_kernel(n, mirrored_ref, a_ref, b_ref, got_ref, out_ref):
    @pl.when(mirrored_ref[0] == 0)
    def _():
        matrix = forward_matrix(a_ref, b_ref, n)
        both = dot(matrix, jnp.concatenate([got_ref[0:n], unfold(got_ref[n : n + n // 2])], axis=1))
        put_forward_a(out_ref, n, a_ref[0:n] + both[:, 0:LANES], both[:, LANES:])

    @pl.when(mirrored_ref[0] != 0)
    def _():
        join_mirrored(n, HEAD, a_ref, b_ref, got_ref, out_ref)


def join_b_kernel(n, mirrored_ref, a_ref, b_ref, got_ref, out_ref):
    @pl.when(mirrored_ref[0] == 0)
    def _():
        matrix = forward_matrix(a_ref, b_ref, n)
        both = dot(matrix, jnp.concatenate([got_ref[0:n], got_ref[n : 2 * n]], axis=1))
        put_forward_b(out_ref, n, both[:, 0:LANES], both[:, LANES:])

    @pl.when(mirrored_ref[0] != 0)
    def _():
        join_mirrored(n, n - HEAD, a_ref, b_ref, got_ref, out_ref)


def first_join_a_kernel(n, mirrored_ref, both_ref, got_ref, out_ref):
    join_a_kernel(n, mirrored_ref, *chunks(both_ref, n), chunks(got_ref, n)[0], out_ref)


def first_join_b_kernel(n, mirrored_ref, both_ref, got_ref, out_ref):
    join_b_kernel(n, mirrored_ref, *chunks(both_ref, n), chunks(got_ref, n)[1], out_ref)


def split_kernel(n, mirrored_ref, band_ref, a_ref, b_ref, got_ref, new_a_ref, m_ref, s_ref, half_ref):
    m = n + n // 2

    @pl.when(mirrored_ref[0] == 0)
    def _():
        matrix = forward_matrix(a_ref, b_ref, n)
        both = dot(matrix, jnp.concatenate([got_ref[0:n], got_ref[n : 2 * n]], axis=1))
        m_ref[0:n] = both[:, 0:LANES]
        m_ref[n : 2 * n] = both[:, LANES:]
        m_ref[2 * n :] = new_a_ref[n:m]
        s_ref[...] = new_a_ref[0:n]

    @pl.when(mirrored_ref[0] != 0)
    def _():
        got = mirrored_parts(got_ref, n - HEAD)
        own = mirrored_all(a_ref, b_ref, n)
        both = dot(
            jnp.concatenate(got[:3], axis=1), jnp.concatenate([own[0], own[1], own[3], own[2]], axis=1)
        )
        top = mirrored_parts(new_a_ref, HEAD)
        m_ref[0:HEAD] = top[0]
        m_ref[HEAD:n] = both[:, 0:LANES]
        m_ref[n : n + HEAD] = top[1]
        m_ref[n + HEAD : 2 * n] = both[:, LANES : 2 * LANES]
        m_ref[2 * n :] = fold(jnp.concatenate([top[2], both[:, 3 * LANES :]], axis=0))
        s_ref[0:HEAD] = top[3]
        s_ref[HEAD:n] = got[3] + both[:, 2 * LANES : 3 * LANES]

    count = half_ref.shape[0]
    half_ref[...] = m_ref[pl.ds(pl.multiple_of(band_ref[0] * count, 8), count)]


def whole(ref, n):
    return jnp.concatenate([ref[0:n], ref[n : 2 * n], unfold(ref[2 * n :])], axis=1)


def put_halves(band_ref, mine_ref, other_ref, both_ref):
    count = mine_ref.shape[0]
    both_ref[pl.ds(pl.multiple_of(band_ref[0] * count, 8), count)] = mine_ref[...]
    both_ref[pl.ds(pl.multiple_of((1 - band_ref[0]) * count, 8), count)] = other_ref[...]


def forward_kernel(m_ref, s_ref, got_ref, out_ref):
    out_ref[...] = s_ref[...] + dot(whole(m_ref, s_ref.shape[0]), got_ref[...])


def mirrored_kernel(band_ref, s_ref, mine_ref, other_ref, got_ref, out_ref, gotm_ref):
    put_halves(band_ref, mine_ref, other_ref, gotm_ref)
    out_ref[...] = got_ref[...] + dot(whole(gotm_ref, s_ref.shape[0]), s_ref[...])


def square_kernel(mirrored_ref, m_ref, gotm_ref, out_ref):
    n = out_ref.shape[0]

    @pl.when(mirrored_ref[0] == 0)
    def _():
        out_ref[...] = dot(whole(m_ref, n), whole(gotm_ref, n))

    @pl.when(mirrored_ref[0] != 0)
    def _():
        out_ref[...] = dot(whole(gotm_ref, n), whole(m_ref, n))


def close_kernel(m_ref, s_ref, got_ref, flux_ref, out_ref, trace_ref):
    out_ref[...] = s_ref[...] + dot(m_ref[...], got_ref[...])
    trace_ref[...] = dot(flux_ref[...], out_ref[...])


def second_kernel(
    row_ref, m_ref, s_ref, got_ref, ready_ref, moved_ref, early_ref, flux_ref, gain_ref, going_ref, base_ref, out_ref
):
    n = ready_ref.shape[0]
    mirror = row_ref[0] % 2 == 1

    @pl.when(mirror)
    def _():
        going_ref[0:n] = s_ref[...] + dot(m_ref[...], got_ref[...])

    @pl.when(jnp.logical_not(mirror))
    def _():
        going_ref[0:n] = ready_ref[...]

    @pl.when(row_ref[0] == 1)
    def _():
        going_ref[n:] = moved_ref[...]
        base = dot(early_ref[:, 0:n], going_ref[0:n])
        base_ref[...] = base
        out_ref[...] = base + dot(early_ref[:, n:], moved_ref[...])

    @pl.when(row_ref[0] != 1)
    def _():
        going_ref[n:] = jnp.zeros_like(moved_ref)
        base = dot(flux_ref[...], going_ref[0:n])
        base_ref[...] = base
        out_ref[...] = base


def third_kernel(base_ref, gain_ref, moved_ref, out_ref):
    out_ref[...] = base_ref[...] + dot(gain_ref[...], moved_ref[...])


def last_kernel(
    row_ref, going_ref, homed_ref, second_ref, third_ref, lift_ref, flux_ref, gain_ref, state_ref, trace_ref
):
    n = state_ref.shape[1]
    inlets = (going_ref.at[n:], homed_ref.at[n:], second_ref, third_ref)
    for row, inlet_ref in enumerate(inlets):
        held_ref = homed_ref if is_mirrored(row) else going_ref

        @pl.when(row_ref[0] == row)
        def _(held_ref=held_ref, inlet_ref=inlet_ref):
            state, inlet = held_ref[0:n], inlet_ref[...]
            state_ref[0] = state + dot(lift_ref[...], inlet, (0, 0))
            trace_ref[0] = dot(flux_ref[...], state) + dot(gain_ref[...], inlet)


VMEM = pl.BlockSpec(memory_space=pltpu.VMEM)
SMEM = pl.BlockSpec(memory_space=pltpu.SMEM)
HBM = pl.BlockSpec(memory_space=pltpu.HBM)


def call(kernel, specs, shapes, *operands, scratch=()):
    shapes = [jax.ShapeDtypeStruct(shape, jnp.float32) for shape in shapes]
    out = pl.pallas_call(
        kernel,
        out_shape=shapes,
        in_specs=specs,
        out_specs=[VMEM] * len(shapes),
        scratch_shapes=scratch,
        compiler_params=pltpu.CompilerParams(vmem_limit_bytes=12 << 20),
    )(*operands)
    return out[0] if len(shapes) == 1 else out


def sector_route(rows, sectors, step):
    return [
        (row * sectors + s, row * sectors + (s + step(row)) % sectors)
        for row in range(rows)
        if step(row) is not None
        for s in range(sectors)
    ]


def is_mirrored(row):
    return row % 2 == 1


def hop(trace, shift, senders, sectors):
    def send(step, trace):
        route = [
            (row * sectors + s, (row + 1) * sectors + (s + step) % sectors)
            for row in senders
            for s in range(sectors)
        ]
        return lax.ppermute(trace, ("row", "sector"), route)

    return lax.switch(shift & (FINE - 1), [functools.partial(send, k) for k in range(FINE)], trace)


def turn(trace, shift, rows, sectors):
    def send(step, trace):
        if step == 0:
            return trace
        route = sector_route(rows, sectors, lambda row: None if is_mirrored(row) else step)
        return lax.ppermute(trace, ("row", "sector"), route)

    steps = [functools.partial(send, k) for k in range(0, sectors, FINE)]
    return lax.switch(shift >> 2, steps, trace)


def on_device(residual, block_inverse, cycle_coupling, outlet_flux, inlet_lift, mortar_shift):
    flux = outlet_flux[0, 0, 0]
    lift = inlet_lift[0, 0, 0]
    n = cycle_coupling.shape[-1]
    rows = lax.axis_size("row")
    row_index = lax.axis_index("row")
    sectors = lax.axis_size("sector")
    last = sectors.bit_length() - 2
    half = sectors // 2
    axes = ("row", "sector")
    mirror = is_mirrored(row_index)
    mirrored = jnp.reshape(mirror, (1,)).astype(jnp.int32)
    rows_a, rows_b = [(count, LANES) for count in chunk_rows(n)]

    def move(block, step):
        route = sector_route(rows, sectors, lambda row: -step if is_mirrored(row) else step)
        return lax.ppermute(block, axes, route)

    start = call(
        first_kernel,
        [SMEM, HBM, HBM, HBM],
        [(rows_a[0] + rows_b[0], LANES)],
        mirrored,
        *[
            pltpu.with_memory_space_constraint(block, pltpu.HBM)
            for block in (block_inverse[0, 0, 0], residual[0, 0, 0], cycle_coupling[0, 0])
        ],
        scratch=[
            pltpu.VMEM((n, n), jnp.float32),
            pltpu.VMEM((n, LANES), jnp.float32),
            pltpu.VMEM((n, n), jnp.float32),
            pltpu.SemaphoreType.DMA((3,)),
        ],
    )
    join_a = functools.partial(join_a_kernel, n)
    join_b = functools.partial(join_b_kernel, n)

    def step(kernel, shapes, *blocks):
        return call(kernel, [SMEM] + [VMEM] * len(blocks), shapes, mirrored, *blocks)

    got = move(start, 1)
    gain = exact_dot(flux, lift)
    early = lax.ppermute(
        jnp.concatenate([flux, gain], axis=1),
        axes,
        sector_route(rows, sectors, lambda row: 1 - half if row == 1 else None),
    )
    a = step(functools.partial(first_join_a_kernel, n), [rows_a], start, got)
    got_a = move(a, 2)
    b = step(functools.partial(first_join_b_kernel, n), [rows_b], start, got)
    got_b = move(b, 2)
    for level in range(2, last - 1):
        new_a = step(join_a, [rows_a], a, b, got_a)
        next_a = move(new_a, 2**level)
        got_b = lax.optimization_barrier((got_b, new_a))[0]
        new_b = step(join_b, [rows_b], a, b, got_b)
        next_b = move(new_b, 2**level)
        a, b, got_a, got_b = new_a, new_b, next_a, next_b

    new_a = step(join_a, [rows_a], a, b, got_a)
    got_b = lax.optimization_barrier((got_b, new_a))[0]
    count = n + n // 4
    band = jnp.reshape(lax.axis_index("band"), (1,)).astype(jnp.int32)
    matrix, state, mine = call(
        functools.partial(split_kernel, n),
        [SMEM] * 2 + [VMEM] * 4,
        [(2 * count, LANES), (n, LANES), (count, LANES)],
        mirrored,
        band,
        a,
        b,
        got_b,
        new_a,
    )
    got = move(state, half // 2)
    got_mine = move(mine, half // 2)
    ahead = call(forward_kernel, [VMEM] * 3, [(n, LANES)], matrix, state, got)
    route = sector_route(rows, sectors, lambda row: None if is_mirrored(row) else half)
    got_ahead = lax.ppermute(ahead, axes, route)
    got_other = lax.ppermute(got_mine, "band", [(0, 1), (1, 0)])
    behind, got_matrix = call(
        mirrored_kernel,
        [SMEM] + [VMEM] * 4,
        [(n, LANES), (2 * count, LANES)],
        band,
        state,
        got_mine,
        got_other,
        got,
    )
    route = sector_route(rows, sectors, lambda row: half if is_mirrored(row) else None)
    got_behind = lax.ppermute(behind, axes, route)
    matrix = step(square_kernel, [(n, n)], matrix, got_matrix)

    mask = sectors - 1
    shifts = [mortar_shift[k] for k in range(rows - 1)]
    face = (flux.shape[0], LANES)
    state, trace = call(
        close_kernel, [VMEM] * 4, [(n, LANES), face], matrix, ahead, got_ahead, flux
    )
    shift = (shifts[0] - (half - 1)) & mask
    moved = hop(turn(trace, shift, rows, sectors), shift, range(0, rows - 1, 2), sectors)

    row = jnp.reshape(row_index, (1,)).astype(jnp.int32)
    going, base, leaving = call(
        second_kernel,
        [SMEM] + [VMEM] * 8,
        [(n + face[0], LANES), face, face],
        row,
        matrix,
        behind,
        got_behind,
        state,
        moved,
        early,
        flux,
        gain,
    )
    shift = (shifts[1] + (half - 1)) & mask
    moved = hop(leaving, shift, range(1, rows - 1, 2), sectors)
    going, moved = lax.optimization_barrier((going, moved))
    route = sector_route(rows, sectors, lambda row: half - 1 if is_mirrored(row) else None)
    homed = lax.ppermute(going, axes, route)
    second = turn(moved, shift, rows, sectors)
    shift = shifts[2] & mask
    leaving = call(third_kernel, [VMEM] * 3, [face], base, gain, second)
    leaving = turn(leaving, shift, rows, sectors)
    third = hop(leaving, shift, range(0, rows - 1, 2), sectors)
    return call(
        last_kernel,
        [SMEM] + [VMEM] * 7,
        [(1, n, LANES), (1,) + face],
        row,
        going,
        homed,
        second,
        third,
        lift.T,
        flux,
        gain,
    )


def solution(mesh):
    in_specs = (
        P("row", "sector", "band", None, None),
        P("row", "sector", "band", None, None),
        P("row", "sector", None, None),
        P("row", "sector", "band", None, None),
        P("row", "sector", "band", None, None),
        P(),
    )
    out_specs = (P("row", "sector", "band", None, None), P("row", "sector", "band", None, None))

    def layer(*operands):
        return tuple(block[None, None] for block in on_device(*operands))

    return jax.shard_map(
        layer, mesh=mesh, in_specs=in_specs, out_specs=out_specs, check_vma=False
    )
```
